32 devices in a mesh: seq: 8 (over z, y), head: 2 (over x), dp: 2 (over core).
Axes of the slice: x: 2, y: 2, z: 4, core: 2. Of those that a mesh axis runs over, the one named last changes fastest.
Arguments:
- queries: bfloat16 [2048, 4096], P(('dp', 'seq'), 'head'), parts along dimension 0, may hold values from -6 to 6
- key_vectors: bfloat16 [2048, 4096], P(('dp', 'seq'), 'head'), parts along dimension 0, may hold values from -6 to 6
- value_vectors: bfloat16 [2048, 4096], P(('dp', 'seq'), 'head'), parts along dimension 0, may hold values from -6 to 6
- grad_out: bfloat16 [2048, 4096], P(('dp', 'seq'), 'head'), parts along dimension 0, may hold values from -6 to 6
Outputs:
- grad_queries: bfloat16 [2048, 4096], P(('dp', 'seq'), 'head'), parts along dimension 0
- grad_keys: bfloat16 [2048, 4096], P(('dp', 'seq'), 'head'), parts along dimension 0
- grad_values: bfloat16 [2048, 4096], P(('dp', 'seq'), 'head'), parts along dimension 0
The draws below stay inside these ranges and needn't reach their ends.
There are 2 independent parts, one for each index of `dp`. The reference program is written for one: setup_inputs(seed, part) draws one part's arguments, and reference() takes and returns one part's arrays. A program takes and returns all parts, laid end to end along the dimension named above; each array names one. Nothing has to cross between parts.
All inputs are finite; a program needn't handle non-finite values.
Results may differ from the reference program's by a relative error of at most 0.012.
Values may be sent and summed in bfloat16 or wider, within the bound.
No kernel may reach another device: no remote copies, remote signals or barrier semaphores. Data moves between devices by JAX's collectives and lax.ppermute only.
A program may use at most 128 MiB of HBM per device.

```python
import jax
import jax.numpy as jnp
from jax import lax

D = 4096
H = 32
E = 128
B = 128
TOKENS = 1024


def paired(key):
    query_out = jnp.clip(jax.random.normal(jax.random.fold_in(key, 21), (TOKENS, D), jnp.float32), -6.0, 6.0)
    key_out = jnp.clip(jax.random.normal(jax.random.fold_in(key, 22), (TOKENS, D), jnp.float32), -6.0, 6.0)
    return (query_out, key_out)


def draw_queries(key, part):
    return paired(key)[0].astype(jnp.bfloat16)


def draw_key_vectors(key, part):
    return paired(key)[1].astype(jnp.bfloat16)


def block_levels(stream_key, dims, pieces, smallest, largest):
    def one(dim, blocks):
        steps = jax.random.uniform(jax.random.fold_in(jax.random.fold_in(stream_key, 6), dim), (blocks,), jnp.float32, smallest / len(pieces), largest / len(pieces))
        return jnp.repeat(jnp.exp(steps), dims[dim] // blocks).reshape((-1,) + (1,) * (len(dims) - dim - 1))

    level = one(*pieces[0])
    for cut in pieces[1:]:
        level = level * one(*cut)
    return level


def centred(own_key, dims, deviation, most, shards=(), kind=jnp.bfloat16):
    factor_of = block_levels(own_key, dims, shards, -0.22, 0.18) if shards else 1.0
    array = jax.random.normal(own_key, dims, jnp.float32) * deviation * factor_of
    return jnp.minimum(jnp.maximum(array, -most), most).astype(kind)


def setup_inputs(seed: int = 0, part: int = 0) -> dict:
    keys = jax.random.split(jax.random.key(seed), 5)
    part_splits = jax.random.split(jax.random.fold_in(keys[4], part), 5)
    queries = draw_queries(jax.random.fold_in(jax.random.fold_in(keys[4], part), 71), part)
    key_vectors = draw_key_vectors(jax.random.fold_in(jax.random.fold_in(keys[4], part), 71), part)
    value_vectors = centred(part_splits[2], (TOKENS, D), 1.0, 6.0, ((0, 8), (1, 2)))
    grad_out = centred(part_splits[3], (TOKENS, D), 1.0, 6.0, ((0, 8), (1, 2)))
    return {"queries": queries, "key_vectors": key_vectors, "value_vectors": value_vectors, "grad_out": grad_out}


masked_value = -1e30


def attend_back(query_part, key_part, value_part, grad_part, allowed):
    scaling = query_part.shape[2] ** -0.5
    query_wide = query_part.astype(jnp.float32)
    key_wide = key_part.astype(jnp.float32)
    value_wide = value_part.astype(jnp.float32)
    grad_wide = grad_part.astype(jnp.float32)
    logits = jnp.einsum("qhe,khe->hqk", query_wide, key_wide) * scaling
    logits = jnp.where(allowed[None], logits, masked_value)
    row_max = jnp.max(logits, axis=2, keepdims=True)
    log_total = row_max + jnp.log(jnp.sum(jnp.exp(logits - row_max), axis=2, keepdims=True))
    probs = jnp.exp(logits - log_total)
    probs_low = lax.optimization_barrier(probs.astype(jnp.bfloat16)).astype(jnp.float32)
    output = jnp.einsum("hqk,khe->qhe", probs_low, value_wide)
    inner_term = jnp.einsum("qhe,qhe->hq", grad_wide, output)[:, :, None]
    grad_probs = jnp.einsum("qhe,khe->hqk", grad_wide, value_wide)
    grad_logits = lax.optimization_barrier((probs * (grad_probs - inner_term)).astype(jnp.bfloat16)).astype(jnp.float32)
    grad_query = scaling * jnp.einsum("hqk,khe->qhe", grad_logits, key_wide)
    grad_keyset = scaling * jnp.einsum("hqk,qhe->khe", grad_logits, query_wide)
    grad_valset = jnp.einsum("hqk,qhe->khe", probs_low, grad_wide)
    return grad_query, grad_keyset, grad_valset


def head_grads(operands):
    query_head, key_head, value_head, grad_head = operands
    block_count = TOKENS // B
    query_blocks = query_head.reshape(block_count, B, 1, E)
    key_blocks = key_head.reshape(block_count, B, 1, E)
    value_blocks = value_head.reshape(block_count, B, 1, E)
    grad_blocks = grad_head.reshape(block_count, B, 1, E)
    empty_block = jnp.zeros((1, B, 1, E), key_head.dtype)
    key_before = jnp.concatenate([empty_block, key_blocks[:-1]], axis=0)
    value_before = jnp.concatenate([empty_block, value_blocks[:-1]], axis=0)
    summary_key = key_blocks[:, B - 1]
    summary_value = value_blocks[:, B - 1]

    def one_block(block_index, query_part, key_prev, key_here, value_prev, value_here, grad_part):
        key_set = jnp.concatenate([key_prev, key_here, summary_key], axis=0)
        value_set = jnp.concatenate([value_prev, value_here, summary_value], axis=0)
        steps_b = jnp.arange(B, dtype=jnp.int32)
        query_pos = block_index * B + steps_b
        key_pos = jnp.concatenate([block_index * B - B + steps_b, block_index * B + steps_b,
                                   jnp.arange(block_count, dtype=jnp.int32) * B + B - 1])
        is_local = jnp.arange(2 * B + block_count, dtype=jnp.int32) < 2 * B
        near = (key_pos[None, :] > query_pos[:, None] - B) & (key_pos[None, :] <= query_pos[:, None]) & (key_pos[None, :] >= 0)
        far_ok = key_pos[None, :] <= query_pos[:, None] - B
        allowed = jnp.where(is_local[None, :], near, far_ok)
        return attend_back(query_part, key_set, value_set, grad_part, allowed)

    grad_query, grad_keyset, grad_valset = jax.vmap(one_block)(
        jnp.arange(block_count, dtype=jnp.int32), query_blocks, key_before, key_blocks,
        value_before, value_blocks, grad_blocks)
    empty_grad = jnp.zeros((1, B, 1, E), jnp.float32)

    def assemble(grad_set):
        own = grad_set[:, B:2 * B] + jnp.concatenate([grad_set[1:, :B], empty_grad], axis=0)
        summary_sum = jnp.sum(grad_set[:, 2 * B:], axis=0)
        own = own.at[:, B - 1].add(summary_sum)
        return own.reshape(TOKENS, 1, E)

    return grad_query.reshape(TOKENS, 1, E), assemble(grad_keyset), assemble(grad_valset)


def reference(queries, key_vectors, value_vectors, grad_out):
    def split_heads(matrix):
        return matrix.reshape(TOKENS, H, E).transpose(1, 0, 2)[:, :, None, :]

    grad_query, grad_key, grad_value = lax.map(
        head_grads, (split_heads(queries), split_heads(key_vectors), split_heads(value_vectors), split_heads(grad_out)))

    def join_heads(stacked):
        return stacked[:, :, 0].transpose(1, 0, 2).reshape(TOKENS, D).astype(jnp.bfloat16)

    return join_heads(grad_query), join_heads(grad_key), join_heads(grad_value)
```

```python
import functools

import jax
import jax.numpy as jnp
from jax import lax
from jax.experimental import pallas as pl
from jax.experimental.pallas import tpu as pltpu
from jax.sharding import PartitionSpec as P

E = 128
B = 128
STAT_ROWS = 16
MASKED = -1e30
F32 = jnp.float32
BF16 = jnp.bfloat16


def dot(a, b, contract):
    return lax.dot_general(a, b, (contract, ((), ())), preferred_element_type=F32)


def heads_per_step(heads):
    return 4 if heads % 4 == 0 else 1


def passed_along(block, distance):
    count = lax.axis_size("seq")
    route = [(i - distance, i) for i in range(count) if 0 <= i - distance < count]
    return lax.ppermute(block, "seq", route)


def own_stats_kernel(group, heads, q_ref, k_ref, v_ref, g_ref, out_ref):
    key = lax.broadcasted_iota(jnp.int32, (B, B), 0)
    query = lax.broadcasted_iota(jnp.int32, (B, B), 1)
    allowed = key <= query
    first = pl.program_id(0) * group
    for j in range(group):
        cols = slice(j * E, (j + 1) * E)
        q, k, v, g = q_ref[:, cols], k_ref[:, cols], v_ref[:, cols], g_ref[:, cols]
        logits = jnp.where(allowed, dot(k, q, ((1,), (1,))) * E**-0.5, MASKED)
        top = jnp.max(logits, axis=0, keepdims=True)
        weight = jnp.exp(logits - top)
        total = jnp.sum(weight, axis=0, keepdims=True)
        inner = jnp.sum(weight * dot(v, g, ((1,), (1,))), axis=0, keepdims=True)
        out_ref[pl.ds(first + j, 1), :] = top + jnp.log(total)
        out_ref[pl.ds(heads + first + j, 1), :] = inner / total


def in_three(x):
    high = x.astype(BF16).astype(F32)
    middle = (x - high).astype(BF16).astype(F32)
    low = (x - high - middle).astype(BF16).astype(F32)
    return [high, middle, low]


def cross_kernel(
    group, heads, count, place_ref, q_ref, g_ref, k_ref, v_ref, stats_ref, summary_ref,
    gq_ref, gk_ref, gv_ref, gs_ref, rows, sums
):
    place = place_ref[0]
    step = pl.program_id(0)
    padded = sums.shape[0] // (2 * heads)
    scale = E**-0.5

    @pl.when(step == 0)
    def _():
        rows[...] = summary_ref[...].astype(F32).reshape(rows.shape)

    key = lax.broadcasted_iota(jnp.int32, (B + padded, B), 0)
    query = lax.broadcasted_iota(jnp.int32, (B + padded, B), 1)
    allowed = ((key < B) & ((key > query) | (key == B - 1))) | ((key >= B) & (key - B < place))

    def summary(row):
        part = rows[pl.ds(row, count, stride=2 * heads), :]
        if padded > count:
            part = jnp.concatenate([part, jnp.zeros((padded - count, E), F32)], axis=0)
        return part.astype(BF16)

    for j in range(group):
        head = step * group + j
        cols = slice(j * E, (j + 1) * E)
        q, g = q_ref[:, cols], g_ref[:, cols]
        k = jnp.concatenate([k_ref[:, cols], summary(head)], axis=0)
        v = jnp.concatenate([v_ref[:, cols], summary(heads + head)], axis=0)
        logits = jnp.where(allowed, dot(k, q, ((1,), (1,))) * scale, MASKED)
        grad_probs = dot(v, g, ((1,), (1,)))
        own_log = stats_ref[pl.ds(head, 1), :]
        own_inner = stats_ref[pl.ds(heads + head, 1), :]
        top = jnp.maximum(jnp.max(logits, axis=0, keepdims=True), own_log)
        weight = jnp.exp(logits - top)
        own_weight = jnp.exp(own_log - top)
        total = own_weight + jnp.sum(weight, axis=0, keepdims=True)
        part = 1.0 / total
        inner = part * (
            own_weight * own_inner + jnp.sum(weight * grad_probs, axis=0, keepdims=True)
        )
        probs = weight * part
        probs_low = probs.astype(BF16)
        grad_logits = (probs * (grad_probs - inner)).astype(BF16)
        gq_ref[:B, cols] = (scale * dot(grad_logits, k, ((0,), (0,)))).astype(BF16)
        stats = in_three(top + jnp.log(total)) + in_three(inner)
        stats.append(jnp.zeros((STAT_ROWS - len(stats), E), F32))
        gq_ref[B:, cols] = jnp.concatenate(stats, axis=0).astype(BF16)
        grad_k = scale * dot(grad_logits, q, ((1,), (0,)))
        grad_v = dot(probs_low, g, ((1,), (0,)))
        gk_ref[:, cols] = grad_k[:B]
        gv_ref[:, cols] = grad_v[:B]
        sums[pl.ds(pl.multiple_of(head * padded, padded), padded), :] = grad_k[B:]
        sums[pl.ds(pl.multiple_of((heads + head) * padded, padded), padded), :] = grad_v[B:]

    @pl.when(step == pl.num_programs(0) - 1)
    def _():
        for t in range(count):
            gs_ref[t] = sums[pl.ds(t, 2 * heads, stride=padded), :]


def final_kernel(
    group, heads, place_ref, q_ref, g_ref, k_ref, v_ref, own_ref, back_ref, gk_ref, gv_ref,
    gs_ref, out_q_ref, out_k_ref, out_v_ref, sums
):
    place = place_ref[0]
    step = pl.program_id(0)
    scale = E**-0.5

    @pl.when(step == 0)
    def _():
        sums[...] = jnp.sum(gs_ref[...], axis=0)

    key = lax.broadcasted_iota(jnp.int32, (B, B), 0)
    query = lax.broadcasted_iota(jnp.int32, (B, B), 1)
    allowed = key <= query
    last_row = key == B - 1
    for j in range(group):
        head = step * group + j
        cols = slice(j * E, (j + 1) * E)
        q, k, v, g = q_ref[:, cols], k_ref[:, cols], v_ref[:, cols], g_ref[:, cols]
        sent = back_ref[B:, cols].astype(F32)
        log_total = sent[0:1] + sent[1:2] + sent[2:3]
        inner = sent[3:4] + sent[4:5] + sent[5:6]
        log_total = jnp.where(place == 0, own_ref[pl.ds(head, 1), :], log_total)
        inner = jnp.where(place == 0, own_ref[pl.ds(heads + head, 1), :], inner)
        logits = jnp.where(allowed, dot(k, q, ((1,), (1,))) * scale, MASKED)
        probs = jnp.exp(logits - log_total)
        probs_low = probs.astype(BF16)
        grad_logits = (probs * (dot(v, g, ((1,), (1,))) - inner)).astype(BF16)
        grad_q = scale * dot(grad_logits, k, ((0,), (0,))) + back_ref[:B, cols].astype(F32)
        grad_k = scale * dot(grad_logits, q, ((1,), (0,))) + gk_ref[:, cols]
        grad_v = dot(probs_low, g, ((1,), (0,))) + gv_ref[:, cols]
        grad_k += jnp.where(last_row, sums[pl.ds(head, 1), :], 0.0)
        grad_v += jnp.where(last_row, sums[pl.ds(heads + head, 1), :], 0.0)
        out_q_ref[:, cols] = grad_q.astype(BF16)
        out_k_ref[:, cols] = grad_k.astype(BF16)
        out_v_ref[:, cols] = grad_v.astype(BF16)


def body(queries, key_vectors, value_vectors, grad_out):
    shard_len, features = queries.shape
    assert shard_len == B
    heads = features // E
    group = heads_per_step(heads)
    steps = heads // group
    count = lax.axis_size("seq")
    padded = -(-count // 16) * 16
    place = lax.axis_index("seq").astype(jnp.int32).reshape(1)

    def columns(rows):
        return pl.BlockSpec((rows, group * E), lambda i, *_: (0, i))

    def whole(*shape):
        return pl.BlockSpec(shape, lambda i, *_: (0,) * len(shape))

    block = columns(B)
    wide = jax.ShapeDtypeStruct((B, features), BF16)
    wide_f32 = jax.ShapeDtypeStruct((B, features), F32)
    flops = 2 * heads * B * B * E

    next_q = passed_along(queries, -1)
    next_g = passed_along(grad_out, -1)

    own_stats = pl.pallas_call(
        functools.partial(own_stats_kernel, group, heads),
        grid=(steps,),
        in_specs=[block] * 4,
        out_specs=whole(2 * heads, B),
        out_shape=jax.ShapeDtypeStruct((2 * heads, B), F32),
        cost_estimate=pl.CostEstimate(
            flops=2 * flops, bytes_accessed=4 * B * features * 2, transcendentals=heads * B * B
        ),
        name="own_stats",
    )(queries, key_vectors, value_vectors, grad_out)
    next_stats = passed_along(own_stats, -1)

    last_rows = jnp.concatenate(
        [key_vectors[B - 1].reshape(heads, E), value_vectors[B - 1].reshape(heads, E)], axis=0
    )
    summary = lax.all_to_all(
        jnp.broadcast_to(last_rows[None], (count, 2 * heads, E)), "seq", 0, 0, tiled=True
    )

    grad_q_next, grad_k, grad_v, grad_summary = pl.pallas_call(
        functools.partial(cross_kernel, group, heads, count),
        grid_spec=pltpu.PrefetchScalarGridSpec(
            num_scalar_prefetch=1,
            grid=(steps,),
            in_specs=[block] * 4 + [whole(2 * heads, B), whole(count, 2 * heads, E)],
            out_specs=[columns(B + STAT_ROWS), block, block, whole(count, 2 * heads, E)],
            scratch_shapes=[
                pltpu.VMEM((count * 2 * heads, E), F32),
                pltpu.VMEM((padded * 2 * heads, E), F32),
            ],
        ),
        out_shape=[
            jax.ShapeDtypeStruct((B + STAT_ROWS, features), BF16),
            wide_f32,
            wide_f32,
            jax.ShapeDtypeStruct((count, 2 * heads, E), F32),
        ],
        cost_estimate=pl.CostEstimate(
            flops=5 * flops, bytes_accessed=9 * B * features * 2, transcendentals=heads * B * B
        ),
        name="cross",
    )(place, next_q, next_g, key_vectors, value_vectors, next_stats, summary)

    back = passed_along(grad_q_next, 1)
    grad_summary = lax.all_to_all(grad_summary, "seq", 0, 0, tiled=True)

    return pl.pallas_call(
        functools.partial(final_kernel, group, heads),
        grid_spec=pltpu.PrefetchScalarGridSpec(
            num_scalar_prefetch=1,
            grid=(steps,),
            in_specs=[block] * 4
            + [
                whole(2 * heads, B),
                columns(B + STAT_ROWS),
                block,
                block,
                whole(count, 2 * heads, E),
            ],
            out_specs=[block] * 3,
            scratch_shapes=[pltpu.VMEM((2 * heads, E), F32)],
        ),
        out_shape=[wide, wide, wide],
        cost_estimate=pl.CostEstimate(
            flops=5 * flops, bytes_accessed=12 * B * features * 2, transcendentals=heads * B * B
        ),
        name="final",
    )(
        place,
        queries,
        grad_out,
        key_vectors,
        value_vectors,
        own_stats,
        back,
        grad_k,
        grad_v,
        grad_summary,
    )


def solution(mesh):
    spec = P(("dp", "seq"), "head")
    return jax.shard_map(
        body,
        mesh=mesh,
        in_specs=(spec,) * 4,
        out_specs=(spec,) * 3,
        check_vma=False,
    )
```

```python
import functools

import jax
import jax.numpy as jnp
from jax import lax
from jax.experimental import pallas as pl
from jax.experimental.pallas import tpu as pltpu
from jax.sharding import PartitionSpec as P

E = 128
B = 128
STAT_ROWS = 16
MASKED = -1e30
F32 = jnp.float32
BF16 = jnp.bfloat16


def dot(a, b, contract):
    return lax.dot_general(a, b, (contract, ((), ())), preferred_element_type=F32)


def passed_along(block, distance):
    count = lax.axis_size("seq")
    route = [(i - distance, i) for i in range(count) if 0 <= i - distance < count]
    return lax.ppermute(block, "seq", route)


def own_stats_kernel(heads, q_ref, k_ref, v_ref, g_ref, out_ref):
    key = lax.broadcasted_iota(jnp.int32, (B, B), 0)
    query = lax.broadcasted_iota(jnp.int32, (B, B), 1)
    allowed = key <= query
    for h in range(heads):
        cols = slice(h * E, (h + 1) * E)
        q, k, v, g = q_ref[:, cols], k_ref[:, cols], v_ref[:, cols], g_ref[:, cols]
        logits = jnp.where(allowed, dot(k, q, ((1,), (1,))) * E**-0.5, MASKED)
        top = jnp.max(logits, axis=0, keepdims=True)
        weight = jnp.exp(logits - top)
        total = jnp.sum(weight, axis=0, keepdims=True)
        inner = jnp.sum(weight * dot(v, g, ((1,), (1,))), axis=0, keepdims=True)
        out_ref[h : h + 1, :] = top + jnp.log(total)
        out_ref[heads + h : heads + h + 1, :] = inner / total


def in_three(x):
    high = x.astype(BF16).astype(F32)
    middle = (x - high).astype(BF16).astype(F32)
    low = (x - high - middle).astype(BF16).astype(F32)
    return [high, middle, low]


def cross_kernel(
    heads, count, place_ref, q_ref, g_ref, k_ref, v_ref, stats_ref, summary_ref,
    gq_ref, gk_ref, gv_ref, gs_ref, rows, sums
):
    place = place_ref[0]
    padded = sums.shape[0] // (2 * heads)
    scale = E**-0.5
    rows[...] = summary_ref[...].astype(F32).reshape(rows.shape)
    key = lax.broadcasted_iota(jnp.int32, (B + padded, B), 0)
    query = lax.broadcasted_iota(jnp.int32, (B + padded, B), 1)
    allowed = ((key < B) & ((key > query) | (key == B - 1))) | ((key >= B) & (key - B < place))

    def summary(row):
        part = rows[pl.ds(row, count, stride=2 * heads), :]
        if padded > count:
            part = jnp.concatenate([part, jnp.zeros((padded - count, E), F32)], axis=0)
        return part.astype(BF16)

    for h in range(heads):
        cols = slice(h * E, (h + 1) * E)
        q, g = q_ref[:, cols], g_ref[:, cols]
        k = jnp.concatenate([k_ref[:, cols], summary(h)], axis=0)
        v = jnp.concatenate([v_ref[:, cols], summary(heads + h)], axis=0)
        logits = jnp.where(allowed, dot(k, q, ((1,), (1,))) * scale, MASKED)
        grad_probs = dot(v, g, ((1,), (1,)))
        own_log = stats_ref[h : h + 1, :]
        own_inner = stats_ref[heads + h : heads + h + 1, :]
        top = jnp.maximum(jnp.max(logits, axis=0, keepdims=True), own_log)
        weight = jnp.exp(logits - top)
        own_weight = jnp.exp(own_log - top)
        total = own_weight + jnp.sum(weight, axis=0, keepdims=True)
        part = 1.0 / total
        inner = part * (
            own_weight * own_inner + jnp.sum(weight * grad_probs, axis=0, keepdims=True)
        )
        probs = weight * part
        probs_low = probs.astype(BF16)
        grad_logits = (probs * (grad_probs - inner)).astype(BF16)
        gq_ref[:B, cols] = (scale * dot(grad_logits, k, ((0,), (0,)))).astype(BF16)
        stats = in_three(top + jnp.log(total)) + in_three(inner)
        stats.append(jnp.zeros((STAT_ROWS - len(stats), E), F32))
        gq_ref[B:, cols] = jnp.concatenate(stats, axis=0).astype(BF16)
        grad_k = scale * dot(grad_logits, q, ((1,), (0,)))
        grad_v = dot(probs_low, g, ((1,), (0,)))
        gk_ref[:, cols] = grad_k[:B]
        gv_ref[:, cols] = grad_v[:B]
        sums[h * padded : (h + 1) * padded, :] = grad_k[B:]
        sums[(heads + h) * padded : (heads + h + 1) * padded, :] = grad_v[B:]

    for t in range(count):
        gs_ref[t] = sums[pl.ds(t, 2 * heads, stride=padded), :]


def final_kernel(
    heads, place_ref, q_ref, g_ref, k_ref, v_ref, own_ref, back_ref, gk_ref, gv_ref,
    gs_ref, out_q_ref, out_k_ref, out_v_ref
):
    first = place_ref[0] == 0
    scale = E**-0.5
    sums = jnp.sum(gs_ref[...], axis=0)
    key = lax.broadcasted_iota(jnp.int32, (B, B), 0)
    query = lax.broadcasted_iota(jnp.int32, (B, B), 1)
    allowed = key <= query
    last_row = key == B - 1
    for h in range(heads):
        cols = slice(h * E, (h + 1) * E)
        q, k, v, g = q_ref[:, cols], k_ref[:, cols], v_ref[:, cols], g_ref[:, cols]
        sent = back_ref[B:, cols].astype(F32)
        log_total = sent[0:1] + sent[1:2] + sent[2:3]
        inner = sent[3:4] + sent[4:5] + sent[5:6]
        log_total = jnp.where(first, own_ref[h : h + 1, :], log_total)
        inner = jnp.where(first, own_ref[heads + h : heads + h + 1, :], inner)
        logits = jnp.where(allowed, dot(k, q, ((1,), (1,))) * scale, MASKED)
        probs = jnp.exp(logits - log_total)
        probs_low = probs.astype(BF16)
        grad_logits = (probs * (dot(v, g, ((1,), (1,))) - inner)).astype(BF16)
        grad_q = scale * dot(grad_logits, k, ((0,), (0,))) + back_ref[:B, cols].astype(F32)
        grad_k = scale * dot(grad_logits, q, ((1,), (0,))) + gk_ref[:, cols]
        grad_v = dot(probs_low, g, ((1,), (0,))) + gv_ref[:, cols]
        grad_k += jnp.where(last_row, sums[h : h + 1, :], 0.0)
        grad_v += jnp.where(last_row, sums[heads + h : heads + h + 1, :], 0.0)
        out_q_ref[:, cols] = grad_q.astype(BF16)
        out_k_ref[:, cols] = grad_k.astype(BF16)
        out_v_ref[:, cols] = grad_v.astype(BF16)


def body(queries, key_vectors, value_vectors, grad_out):
    shard_len, features = queries.shape
    assert shard_len == B
    heads = features // E
    count = lax.axis_size("seq")
    padded = -(-count // 16) * 16
    place = lax.axis_index("seq").astype(jnp.int32).reshape(1)
    vmem = pl.BlockSpec(memory_space=pltpu.VMEM)
    smem = pl.BlockSpec(memory_space=pltpu.SMEM)
    wide = jax.ShapeDtypeStruct((B, features), BF16)
    wide_f32 = jax.ShapeDtypeStruct((B, features), F32)
    flops = 2 * heads * B * B * E
    limit = pltpu.CompilerParams(vmem_limit_bytes=24 << 20)

    next_q = passed_along(queries, -1)
    next_g = passed_along(grad_out, -1)

    own_stats = pl.pallas_call(
        functools.partial(own_stats_kernel, heads),
        in_specs=[vmem] * 4,
        out_specs=vmem,
        out_shape=jax.ShapeDtypeStruct((2 * heads, B), F32),
        compiler_params=limit,
        cost_estimate=pl.CostEstimate(
            flops=2 * flops, bytes_accessed=4 * B * features * 2, transcendentals=heads * B * B
        ),
        name="own_stats",
    )(queries, key_vectors, value_vectors, grad_out)
    next_stats = passed_along(own_stats, -1)

    last_rows = jnp.concatenate(
        [key_vectors[B - 1].reshape(heads, E), value_vectors[B - 1].reshape(heads, E)], axis=0
    )
    summary = lax.all_to_all(
        jnp.broadcast_to(last_rows[None], (count, 2 * heads, E)), "seq", 0, 0, tiled=True
    )

    grad_q_next, grad_k, grad_v, grad_summary = pl.pallas_call(
        functools.partial(cross_kernel, heads, count),
        in_specs=[smem] + [vmem] * 6,
        out_specs=[vmem] * 4,
        scratch_shapes=[
            pltpu.VMEM((count * 2 * heads, E), F32),
            pltpu.VMEM((padded * 2 * heads, E), F32),
        ],
        out_shape=[
            jax.ShapeDtypeStruct((B + STAT_ROWS, features), BF16),
            wide_f32,
            wide_f32,
            jax.ShapeDtypeStruct((count, 2 * heads, E), F32),
        ],
        compiler_params=limit,
        cost_estimate=pl.CostEstimate(
            flops=5 * flops, bytes_accessed=9 * B * features * 2, transcendentals=heads * B * B
        ),
        name="cross",
    )(place, next_q, next_g, key_vectors, value_vectors, next_stats, summary)

    back = passed_along(grad_q_next, 1)
    grad_summary = lax.all_to_all(grad_summary, "seq", 0, 0, tiled=True)

    return pl.pallas_call(
        functools.partial(final_kernel, heads),
        in_specs=[smem] + [vmem] * 9,
        out_specs=[vmem] * 3,
        out_shape=[wide, wide, wide],
        compiler_params=limit,
        cost_estimate=pl.CostEstimate(
            flops=5 * flops, bytes_accessed=12 * B * features * 2, transcendentals=heads * B * B
        ),
        name="final",
    )(
        place,
        queries,
        grad_out,
        key_vectors,
        value_vectors,
        own_stats,
        back,
        grad_k,
        grad_v,
        grad_summary,
    )


def solution(mesh):
    spec = P(("dp", "seq"), "head")
    return jax.shard_map(
        body,
        mesh=mesh,
        in_specs=(spec,) * 4,
        out_specs=(spec,) * 3,
        check_vma=False,
    )
```

```python
import functools

import jax
import jax.numpy as jnp
from jax import lax
from jax.experimental import pallas as pl
from jax.experimental.pallas import tpu as pltpu
from jax.sharding import PartitionSpec as P

E = 128
B = 128
STAT_ROWS = 8
MASKED = -1e30
F32 = jnp.float32
BF16 = jnp.bfloat16


def dot(a, b, contract):
    return lax.dot_general(a, b, (contract, ((), ())), preferred_element_type=F32)


def passed_along(block, distance):
    count = lax.axis_size("seq")
    route = [(i - distance, i) for i in range(count) if 0 <= i - distance < count]
    return lax.ppermute(block, "seq", route)


def in_three(x):
    high = x.astype(BF16).astype(F32)
    middle = (x - high).astype(BF16).astype(F32)
    low = (x - high - middle).astype(BF16).astype(F32)
    return [high, middle, low]


def stat_rows(log_total, inner):
    rows = in_three(log_total) + in_three(inner)
    rows.append(jnp.zeros((STAT_ROWS - len(rows), E), F32))
    return jnp.concatenate(rows, axis=0).astype(BF16)


def stats_of(rows):
    rows = rows.astype(F32)
    return rows[0:1] + rows[1:2] + rows[2:3], rows[3:4] + rows[4:5] + rows[5:6]


def head_columns(head):
    return slice(head * E, (head + 1) * E)


def own_stats_kernel(heads, q_ref, k_ref, v_ref, g_ref, out_ref):
    key = lax.broadcasted_iota(jnp.int32, (B, B), 0)
    query = lax.broadcasted_iota(jnp.int32, (B, B), 1)
    allowed = key <= query
    for h in range(heads):
        cols = head_columns(h)
        q, k, v, g = q_ref[:, cols], k_ref[:, cols], v_ref[:, cols], g_ref[:, cols]
        logits = jnp.where(allowed, dot(k, q, ((1,), (1,))) * E**-0.5, MASKED)
        top = jnp.max(logits, axis=0, keepdims=True)
        weight = jnp.exp(logits - top)
        total = jnp.sum(weight, axis=0, keepdims=True)
        inner = jnp.sum(weight * dot(v, g, ((1,), (1,))), axis=0, keepdims=True)
        out_ref[:B, cols] = g
        out_ref[B:, cols] = stat_rows(top + jnp.log(total), inner / total)


def cross_kernel(
    heads, count, place_ref, q_ref, g_ref, k_ref, v_ref, summary_ref,
    gq_ref, gk_ref, gv_ref, gs_ref, sums, low, grads
):
    place = place_ref[0]
    pairs = summary_ref.shape[2]
    padded = low.shape[1] - B
    scale = E**-0.5
    key = lax.broadcasted_iota(jnp.int32, (B + padded, B), 0)
    query = lax.broadcasted_iota(jnp.int32, (B + padded, B), 1)
    same, other = key - B, key - B - pairs
    pair = lax.shift_right_logical(place, 1)
    allowed = (key < B) & ((key > query) | (key == B - 1))
    allowed |= (same >= 1) & (same < pairs) & (same <= pair)
    allowed |= (other >= 1 - (place & 1)) & (other < pairs) & (other <= pair)

    def with_summary(block, which, cols):
        parts = [summary_ref[i, which, :, cols].astype(F32) for i in range(2)]
        if padded > 2 * pairs:
            parts.append(jnp.zeros((padded - 2 * pairs, E), F32))
        return jnp.concatenate([block, jnp.concatenate(parts, axis=0).astype(BF16)], axis=0)

    for h in range(heads):
        cols = head_columns(h)
        k = with_summary(k_ref[:, cols], 0, cols)
        v = with_summary(v_ref[:, cols], 1, cols)
        logits = jnp.where(allowed, dot(k, q_ref[:, cols], ((1,), (1,))) * scale, MASKED)
        grad_probs = dot(v, g_ref[:B, cols], ((1,), (1,)))
        own_log, own_inner = stats_of(g_ref[B:, cols])
        top = jnp.maximum(jnp.max(logits, axis=0, keepdims=True), own_log)
        weight = jnp.exp(logits - top)
        own_weight = jnp.exp(own_log - top)
        total = own_weight + jnp.sum(weight, axis=0, keepdims=True)
        part = 1.0 / total
        inner = part * (
            own_weight * own_inner + jnp.sum(weight * grad_probs, axis=0, keepdims=True)
        )
        probs = weight * part
        low[h] = probs.astype(BF16)
        grads[h] = (probs * (grad_probs - inner)).astype(BF16)
        gq_ref[B:, cols] = stat_rows(top + jnp.log(total), inner)

    for h in range(heads):
        cols = head_columns(h)
        grad_logits = grads[h]
        k = with_summary(k_ref[:, cols], 0, cols)
        gq_ref[:B, cols] = (scale * dot(grad_logits, k, ((0,), (0,)))).astype(BF16)
        grad_k = scale * dot(grad_logits, q_ref[:, cols], ((1,), (0,)))
        grad_v = dot(low[h], g_ref[:B, cols], ((1,), (0,)))
        gk_ref[:, cols] = grad_k[:B]
        gv_ref[:, cols] = grad_v[:B]
        sums[h * padded : (h + 1) * padded, :] = grad_k[B:]
        sums[(heads + h) * padded : (heads + h + 1) * padded, :] = grad_v[B:]

    for t in range(count):
        row = ((place ^ t) & 1) * pairs + pair - t // 2
        row = jnp.where(t < place, row, 0)
        gs_ref[t] = sums[pl.ds(row, 2 * heads, stride=padded), :]


def final_kernel(
    heads, place_ref, q_ref, g_ref, k_ref, v_ref, own_ref, back_ref, gk_ref, gv_ref,
    gs_ref, out_q_ref, out_k_ref, out_v_ref, low, grads, done_q, done_k, done_v, sems
):
    first = place_ref[0] == 0
    scale = E**-0.5
    group = heads // 4 if heads % 4 == 0 else heads
    sums = jnp.sum(gs_ref[...], axis=0)
    key = lax.broadcasted_iota(jnp.int32, (B, B), 0)
    query = lax.broadcasted_iota(jnp.int32, (B, B), 1)
    allowed = key <= query
    last_row = key == B - 1
    for h in range(heads):
        cols = head_columns(h)
        log_total, inner = stats_of(jnp.where(first, own_ref[B:, cols], back_ref[B:, cols]))
        logits = dot(k_ref[:, cols], q_ref[:, cols], ((1,), (1,))) * scale
        probs = jnp.exp(jnp.where(allowed, logits, MASKED) - log_total)
        low[h] = probs.astype(BF16)
        grad_probs = dot(v_ref[:, cols], g_ref[:, cols], ((1,), (1,)))
        grads[h] = (probs * (grad_probs - inner)).astype(BF16)

    copies = []
    for h in range(heads):
        cols = head_columns(h)
        grad_logits = grads[h]
        grad_q = scale * dot(grad_logits, k_ref[:, cols], ((0,), (0,)))
        grad_k = scale * dot(grad_logits, q_ref[:, cols], ((1,), (0,)))
        grad_v = dot(low[h], g_ref[:, cols], ((1,), (0,)))
        grad_k += gk_ref[:, cols] + jnp.where(last_row, sums[h : h + 1, :], 0.0)
        grad_v += gv_ref[:, cols] + jnp.where(last_row, sums[heads + h : heads + h + 1, :], 0.0)
        done_q[:, cols] = (grad_q + back_ref[:B, cols].astype(F32)).astype(BF16)
        done_k[:, cols] = grad_k.astype(BF16)
        done_v[:, cols] = grad_v.astype(BF16)
        if (h + 1) % group == 0:
            part = slice((h + 1 - group) * E, (h + 1) * E)
            for done, out in (done_q, out_q_ref), (done_k, out_k_ref), (done_v, out_v_ref):
                copies.append(
                    pltpu.make_async_copy(
                        done.at[:, part], out.at[:, part], sems.at[len(copies)]
                    )
                )
                copies[-1].start()
    for copy in copies:
        copy.wait()


def body(queries, key_vectors, value_vectors, grad_out):
    shard_len, features = queries.shape
    assert shard_len == B and lax.axis_size("seq") % 2 == 0
    heads = features // E
    count = lax.axis_size("seq")
    place = lax.axis_index("seq").astype(jnp.int32).reshape(1)
    vmem = pl.BlockSpec(memory_space=pltpu.VMEM)
    smem = pl.BlockSpec(memory_space=pltpu.SMEM)
    anywhere = pl.BlockSpec(memory_space=pl.ANY)
    wide = jax.ShapeDtypeStruct((B, features), BF16)
    wide_stats = jax.ShapeDtypeStruct((B + STAT_ROWS, features), BF16)
    wide_f32 = jax.ShapeDtypeStruct((B, features), F32)
    flops = 2 * heads * B * B * E
    limit = pltpu.CompilerParams(vmem_limit_bytes=24 << 20)

    next_q = passed_along(queries, -1)

    rows = jnp.stack([key_vectors[B - 1 :], value_vectors[B - 1 :]])
    swap = lax.ppermute(rows, "seq", [(i, i ^ 1) for i in range(count)])
    summary = jnp.stack([rows, swap])
    while 2 * summary.shape[2] < count:
        earlier = passed_along(summary, 2 * summary.shape[2])
        summary = jnp.concatenate([summary, earlier], axis=2)
    padded = -(-2 * summary.shape[2] // 16) * 16
    _, grad_out = lax.optimization_barrier((swap, grad_out))

    grad_stats = pl.pallas_call(
        functools.partial(own_stats_kernel, heads),
        in_specs=[vmem] * 4,
        out_specs=vmem,
        out_shape=wide_stats,
        compiler_params=limit,
        cost_estimate=pl.CostEstimate(
            flops=2 * flops, bytes_accessed=4 * B * features * 2, transcendentals=heads * B * B
        ),
        name="own_stats",
    )(queries, key_vectors, value_vectors, grad_out)
    next_g = passed_along(grad_stats, -1)

    grad_q_next, grad_k, grad_v, grad_summary = pl.pallas_call(
        functools.partial(cross_kernel, heads, count),
        in_specs=[smem] + [vmem] * 5,
        out_specs=[vmem] * 4,
        scratch_shapes=[
            pltpu.VMEM((padded * 2 * heads, E), F32),
            pltpu.VMEM((heads, B + padded, B), BF16),
            pltpu.VMEM((heads, B + padded, B), BF16),
        ],
        out_shape=[
            wide_stats,
            wide_f32,
            wide_f32,
            jax.ShapeDtypeStruct((count, 2 * heads, E), F32),
        ],
        compiler_params=limit,
        cost_estimate=pl.CostEstimate(
            flops=5 * flops, bytes_accessed=9 * B * features * 2, transcendentals=heads * B * B
        ),
        name="cross",
    )(place, next_q, next_g, key_vectors, value_vectors, summary)

    back = passed_along(grad_q_next, 1)
    grad_summary = lax.all_to_all(grad_summary, "seq", 0, 0, tiled=True)

    return pl.pallas_call(
        functools.partial(final_kernel, heads),
        in_specs=[smem] + [vmem] * 9,
        out_specs=[anywhere] * 3,
        out_shape=[wide, wide, wide],
        scratch_shapes=[
            pltpu.VMEM((heads, B, B), BF16),
            pltpu.VMEM((heads, B, B), BF16),
            pltpu.VMEM((B, features), BF16),
            pltpu.VMEM((B, features), BF16),
            pltpu.VMEM((B, features), BF16),
            pltpu.SemaphoreType.DMA((12,)),
        ],
        compiler_params=limit,
        cost_estimate=pl.CostEstimate(
            flops=5 * flops, bytes_accessed=12 * B * features * 2, transcendentals=heads * B * B
        ),
        name="final",
    )(
        place,
        queries,
        grad_out,
        key_vectors,
        value_vectors,
        grad_stats,
        back,
        grad_k,
        grad_v,
        grad_summary,
    )


def solution(mesh):
    spec = P(("dp", "seq"), "head")
    return jax.shard_map(
        body,
        mesh=mesh,
        in_specs=(spec,) * 4,
        out_specs=(spec,) * 3,
        check_vma=False,
    )
```

```python
import functools

import jax
import jax.numpy as jnp
from jax import lax
from jax.experimental import pallas as pl
from jax.experimental.pallas import tpu as pltpu
from jax.sharding import PartitionSpec as P

E = 128
B = 128
STAT_ROWS = 8
MASKED = -1e30
F32 = jnp.float32
BF16 = jnp.bfloat16


def dot(a, b, contract):
    return lax.dot_general(a, b, (contract, ((), ())), preferred_element_type=F32)


def passed_along(block, distance):
    count = lax.axis_size("seq")
    route = [(i - distance, i) for i in range(count) if 0 <= i - distance < count]
    return lax.ppermute(block, "seq", route)


def in_three(x):
    high = x.astype(BF16).astype(F32)
    middle = (x - high).astype(BF16).astype(F32)
    low = (x - high - middle).astype(BF16).astype(F32)
    return [high, middle, low]


def stat_rows(log_total, inner):
    rows = in_three(log_total) + in_three(inner)
    rows.append(jnp.zeros((STAT_ROWS - len(rows), E), F32))
    return jnp.concatenate(rows, axis=0).astype(BF16)


def stats_of(rows):
    rows = rows.astype(F32)
    return rows[0:1] + rows[1:2] + rows[2:3], rows[3:4] + rows[4:5] + rows[5:6]


def head_columns(head):
    return slice(head * E, (head + 1) * E)


def own_kernel(
    heads, q_ref, k_ref, v_ref, g_ref, out_ref, stats_ref, weight_ref, gp_ref, top_ref
):
    key = lax.broadcasted_iota(jnp.int32, (B, B), 0)
    query = lax.broadcasted_iota(jnp.int32, (B, B), 1)
    allowed = key <= query
    for h in range(heads):
        cols = head_columns(h)
        q, k, v, g = q_ref[:, cols], k_ref[:, cols], v_ref[:, cols], g_ref[:, cols]
        logits = jnp.where(allowed, dot(k, q, ((1,), (1,))) * E**-0.5, MASKED)
        top = jnp.max(logits, axis=0, keepdims=True)
        weight = jnp.exp(logits - top)
        grad_probs = dot(v, g, ((1,), (1,)))
        total = jnp.sum(weight, axis=0, keepdims=True)
        inner = jnp.sum(weight * grad_probs, axis=0, keepdims=True)
        out_ref[:B, cols] = g
        stats = stat_rows(top + jnp.log(total), inner / total)
        out_ref[B:, cols] = stats
        stats_ref[:, cols] = stats
        weight_ref[h] = weight
        gp_ref[h] = grad_probs
        top_ref[h : h + 1, :] = top


def with_summary(block, summary_ref, which, cols, padded):
    pairs = summary_ref.shape[2]
    parts = [summary_ref[i, which, :, cols].astype(F32) for i in range(2)]
    if padded > 2 * pairs:
        parts.append(jnp.zeros((padded - 2 * pairs, E), F32))
    return jnp.concatenate([block, jnp.concatenate(parts, axis=0).astype(BF16)], axis=0)


def cross_weights_kernel(heads, padded, place_ref, q_ref, k_ref, summary_ref, weight_ref, sums_ref):
    place = place_ref[0]
    pairs = summary_ref.shape[2]
    key = lax.broadcasted_iota(jnp.int32, (B + padded, B), 0)
    query = lax.broadcasted_iota(jnp.int32, (B + padded, B), 1)
    same, other = key - B, key - B - pairs
    pair = lax.shift_right_logical(place, 1)
    allowed = (key < B) & ((key > query) | (key == B - 1))
    allowed |= (same >= 1) & (same < pairs) & (same <= pair)
    allowed |= (other >= 1 - (place & 1)) & (other < pairs) & (other <= pair)
    for h in range(heads):
        cols = head_columns(h)
        k = with_summary(k_ref[:, cols], summary_ref, 0, cols, padded)
        logits = jnp.where(allowed, dot(k, q_ref[:, cols], ((1,), (1,))) * E**-0.5, MASKED)
        top = jnp.max(logits, axis=0, keepdims=True)
        weight = jnp.exp(logits - top)
        weight_ref[h] = weight
        sums_ref[h : h + 1, :] = top
        sums_ref[heads + h : heads + h + 1, :] = jnp.sum(weight, axis=0, keepdims=True)


def cross_scores_kernel(
    heads, padded, q_ref, g_ref, v_ref, summary_ref, weight_ref, sums_ref,
    low_ref, grads_ref, stats_ref, same_ref, other_ref
):
    pairs = summary_ref.shape[2]
    scale = E**-0.5
    for h in range(heads):
        cols = head_columns(h)
        v = with_summary(v_ref[:, cols], summary_ref, 1, cols, padded)
        grad_probs = dot(v, g_ref[:B, cols], ((1,), (1,)))
        own_log, own_inner = stats_of(g_ref[B:, cols])
        cross_top = sums_ref[h : h + 1, :]
        weight = weight_ref[h]
        top = jnp.maximum(cross_top, own_log)
        own_weight = jnp.exp(own_log - top)
        cross_weight = jnp.exp(cross_top - top)
        total = own_weight + cross_weight * sums_ref[heads + h : heads + h + 1, :]
        own_part = own_weight / total
        cross_part = cross_weight / total
        inner = own_part * own_inner + cross_part * jnp.sum(
            weight * grad_probs, axis=0, keepdims=True
        )
        probs = weight * cross_part
        low_ref[h] = probs.astype(BF16)
        grads_ref[h] = (probs * (grad_probs - inner)).astype(BF16)
        stats_ref[:, cols] = stat_rows(top + jnp.log(total), inner)
    for h in range(heads):
        cols = head_columns(h)
        grad_k = scale * dot(grads_ref[h, B:, :], q_ref[:, cols], ((1,), (0,)))
        grad_v = dot(low_ref[h, B:, :], g_ref[:B, cols], ((1,), (0,)))
        for i, grad in enumerate((grad_k, grad_v)):
            same_ref[i, :, cols] = grad[:pairs]
            other_ref[i, :, cols] = grad[pairs : 2 * pairs]


def cross_queries_kernel(heads, padded, k_ref, summary_ref, grads_ref, stats_ref, gq_ref):
    gq_ref[B:, :] = stats_ref[...]
    for h in range(heads):
        cols = head_columns(h)
        k = with_summary(k_ref[:, cols], summary_ref, 0, cols, padded)
        gq_ref[:B, cols] = (E**-0.5 * dot(grads_ref[h], k, ((0,), (0,)))).astype(BF16)


def cross_keys_kernel(heads, q_ref, g_ref, low_ref, grads_ref, gk_ref, gv_ref):
    for h in range(heads):
        cols = head_columns(h)
        gk_ref[:, cols] = E**-0.5 * dot(grads_ref[h, :B, :], q_ref[:, cols], ((1,), (0,)))
        gv_ref[:, cols] = dot(low_ref[h, :B, :], g_ref[:B, cols], ((1,), (0,)))


def final_kernel(
    heads, place_ref, q_ref, g_ref, k_ref, own_ref, weight_ref, gp_ref, top_ref, back_ref,
    gk_ref, gv_ref, gs_ref, out_q_ref, out_k_ref, out_v_ref,
    low, grads, done_q, done_k, done_v, sems
):
    first = place_ref[0] == 0
    scale = E**-0.5
    group = heads // 4 if heads % 4 == 0 else heads
    last_row = lax.broadcasted_iota(jnp.int32, (B, B), 0) == B - 1
    for h in range(heads):
        cols = head_columns(h)
        log_total, inner = stats_of(jnp.where(first, own_ref[:, cols], back_ref[B:, cols]))
        probs = weight_ref[h] * jnp.exp(top_ref[h : h + 1, :] - log_total)
        low[h] = probs.astype(BF16)
        grads[h] = (probs * (gp_ref[h] - inner)).astype(BF16)

    copies = []
    for h in range(heads):
        cols = head_columns(h)
        grad_logits = grads[h]
        grad_q = scale * dot(grad_logits, k_ref[:, cols], ((0,), (0,)))
        grad_k = scale * dot(grad_logits, q_ref[:, cols], ((1,), (0,)))
        grad_v = dot(low[h], g_ref[:, cols], ((1,), (0,)))
        grad_k += gk_ref[:, cols] + jnp.where(last_row, gs_ref[0, :, cols], 0.0)
        grad_v += gv_ref[:, cols] + jnp.where(last_row, gs_ref[1, :, cols], 0.0)
        done_q[:, cols] = (grad_q + back_ref[:B, cols].astype(F32)).astype(BF16)
        done_k[:, cols] = grad_k.astype(BF16)
        done_v[:, cols] = grad_v.astype(BF16)
        if (h + 1) % group == 0:
            part = slice((h + 1 - group) * E, (h + 1) * E)
            for done, out in (done_q, out_q_ref), (done_k, out_k_ref), (done_v, out_v_ref):
                copies.append(
                    pltpu.make_async_copy(
                        done.at[:, part], out.at[:, part], sems.at[len(copies)]
                    )
                )
                copies[-1].start()
    for copy in copies:
        copy.wait()


def body(queries, key_vectors, value_vectors, grad_out):
    shard_len, features = queries.shape
    count = lax.axis_size("seq")
    assert shard_len == B and count % 2 == 0
    heads = features // E
    place = lax.axis_index("seq").astype(jnp.int32).reshape(1)
    vmem = pl.BlockSpec(memory_space=pltpu.VMEM)
    smem = pl.BlockSpec(memory_space=pltpu.SMEM)
    anywhere = pl.BlockSpec(memory_space=pl.ANY)

    def kernel(function, name, products, inputs, outputs, spec=vmem, scratch=(), scalar=False):
        out_shape = [jax.ShapeDtypeStruct(shape, kind) for shape, kind in outputs]
        moved = sum(x.size * x.dtype.itemsize for x in (*inputs, *out_shape))
        return pl.pallas_call(
            function,
            in_specs=[smem] * scalar + [vmem] * (len(inputs) - scalar),
            out_specs=[spec] * len(out_shape),
            out_shape=out_shape,
            scratch_shapes=scratch,
            compiler_params=pltpu.CompilerParams(vmem_limit_bytes=16 << 20),
            cost_estimate=pl.CostEstimate(
                flops=products * 2 * heads * B * B * E,
                bytes_accessed=moved,
                transcendentals=heads * B * B,
            ),
            name=name,
        )(*inputs)

    rows = jnp.stack([key_vectors[B - 1 :], value_vectors[B - 1 :]])
    grad_stats, own_stats, weight, grad_probs, top = kernel(
        functools.partial(own_kernel, heads),
        "own",
        2,
        (queries, key_vectors, value_vectors, grad_out),
        [
            ((B + STAT_ROWS, features), BF16),
            ((STAT_ROWS, features), BF16),
            ((heads, B, B), F32),
            ((heads, B, B), F32),
            ((heads, B), F32),
        ],
    )

    across = [(i, i ^ 1) for i in range(count)]
    swap = lax.ppermute(rows, "seq", across)
    rows, queries = lax.optimization_barrier((rows, queries))
    next_q = passed_along(queries, -1)
    summary = jnp.stack([rows, swap])
    _, grad_stats = lax.optimization_barrier((swap, grad_stats))
    while 2 * summary.shape[2] < count:
        earlier = passed_along(summary, 2 * summary.shape[2])
        summary = jnp.concatenate([summary, earlier], axis=2)
    pairs = summary.shape[2]
    padded = -(-2 * pairs // 16) * 16
    next_g = passed_along(grad_stats, -1)

    wide = heads, B + padded, B
    cross_weight, cross_sums = kernel(
        functools.partial(cross_weights_kernel, heads, padded),
        "cross_weights",
        1,
        (place, next_q, key_vectors, summary),
        [(wide, F32), ((2 * heads, B), F32)],
        scalar=True,
    )
    low, grads, stats, same, other = kernel(
        functools.partial(cross_scores_kernel, heads, padded),
        "cross_scores",
        2,
        (next_q, next_g, value_vectors, summary, cross_weight, cross_sums),
        [
            (wide, BF16),
            (wide, BF16),
            ((STAT_ROWS, features), BF16),
            ((2, pairs, features), F32),
            ((2, pairs, features), F32),
        ],
    )
    other = lax.ppermute(other, "seq", across)
    (grad_q_next,) = kernel(
        functools.partial(cross_queries_kernel, heads, padded),
        "cross_queries",
        1,
        (key_vectors, summary, grads, stats),
        [((B + STAT_ROWS, features), BF16)],
    )
    back = passed_along(grad_q_next, 1)
    grad_k, grad_v = kernel(
        functools.partial(cross_keys_kernel, heads),
        "cross_keys",
        2,
        (next_q, next_g, low, grads),
        [((B, features), F32)] * 2,
    )
    grad_summary = same + other
    while pairs > 1:
        ways = 4 if pairs % 4 == 0 else 2
        pairs //= ways
        parts = [grad_summary[:, i * pairs : (i + 1) * pairs] for i in range(ways)]
        sent = [passed_along(parts[i], -2 * pairs * i) for i in range(1, ways)]
        grad_summary = sum(sent, parts[0])

    return kernel(
        functools.partial(final_kernel, heads),
        "final",
        3,
        (
            place,
            queries,
            grad_out,
            key_vectors,
            own_stats,
            weight,
            grad_probs,
            top,
            back,
            grad_k,
            grad_v,
            grad_summary,
        ),
        [((B, features), BF16)] * 3,
        spec=anywhere,
        scratch=[
            pltpu.VMEM((heads, B, B), BF16),
            pltpu.VMEM((heads, B, B), BF16),
            pltpu.VMEM((B, features), BF16),
            pltpu.VMEM((B, features), BF16),
            pltpu.VMEM((B, features), BF16),
            pltpu.SemaphoreType.DMA((12,)),
        ],
        scalar=True,
    )


def solution(mesh):
    spec = P(("dp", "seq"), "head")
    return jax.shard_map(
        body,
        mesh=mesh,
        in_specs=(spec,) * 4,
        out_specs=(spec,) * 3,
        check_vma=False,
    )
```

```python
import functools

import jax
import jax.numpy as jnp
from jax import lax
from jax.experimental import pallas as pl
from jax.experimental.pallas import tpu as pltpu
from jax.sharding import PartitionSpec as P

E = 128
B = 128
STAT_ROWS = 8
MASKED = -1e30
F32 = jnp.float32
BF16 = jnp.bfloat16


def dot(a, b, contract):
    return lax.dot_general(a, b, (contract, ((), ())), preferred_element_type=F32)


def passed_along(block, distance):
    count = lax.axis_size("seq")
    route = [(i - distance, i) for i in range(count) if 0 <= i - distance < count]
    return lax.ppermute(block, "seq", route)


def passed_round(block, distance):
    count = lax.axis_size("seq")
    return lax.ppermute(block, "seq", [(i, (i + distance) % count) for i in range(count)])


def in_three(x):
    high = x.astype(BF16).astype(F32)
    middle = (x - high).astype(BF16).astype(F32)
    low = (x - high - middle).astype(BF16).astype(F32)
    return [high, middle, low]


def stat_rows(log_total, inner):
    rows = in_three(log_total) + in_three(inner)
    rows.append(jnp.zeros((STAT_ROWS - len(rows), E), F32))
    return jnp.concatenate(rows, axis=0).astype(BF16)


def stats_of(rows):
    rows = rows.astype(F32)
    return rows[0:1] + rows[1:2] + rows[2:3], rows[3:4] + rows[4:5] + rows[5:6]


def head_columns(head):
    return slice(head * E, (head + 1) * E)


def own_kernel(
    heads, q_hbm, k_hbm, v_hbm, g_hbm, out_ref, stats_ref, q_ref, k_ref, v_ref, g_ref, sems
):
    group = heads // 4 if heads % 4 == 0 else heads
    pairs = (q_hbm, q_ref), (k_hbm, k_ref), (v_hbm, v_ref), (g_hbm, g_ref)
    copies = []
    for start in range(0, heads, group):
        part = slice(start * E, (start + group) * E)
        for source, target in pairs:
            copies.append(
                pltpu.make_async_copy(
                    source.at[:, part], target.at[:, part], sems.at[len(copies)]
                )
            )
            copies[-1].start()
    key = lax.broadcasted_iota(jnp.int32, (B, B), 0)
    query = lax.broadcasted_iota(jnp.int32, (B, B), 1)
    allowed = key <= query
    for h in range(heads):
        if h % group == 0:
            for copy in copies[h // group * 4 : h // group * 4 + 4]:
                copy.wait()
        cols = head_columns(h)
        q, k, v, g = q_ref[:, cols], k_ref[:, cols], v_ref[:, cols], g_ref[:, cols]
        logits = jnp.where(allowed, dot(k, q, ((1,), (1,))) * E**-0.5, MASKED)
        top = jnp.max(logits, axis=0, keepdims=True)
        weight = jnp.exp(logits - top)
        grad_probs = dot(v, g, ((1,), (1,)))
        total = jnp.sum(weight, axis=0, keepdims=True)
        inner = jnp.sum(weight * grad_probs, axis=0, keepdims=True)
        out_ref[:B, cols] = g
        stats = stat_rows(top + jnp.log(total), inner / total)
        out_ref[B:, cols] = stats
        stats_ref[:, cols] = stats


def own_weights_kernel(heads, q_ref, k_ref, v_ref, g_ref, weight_ref, gp_ref, top_ref):
    key = lax.broadcasted_iota(jnp.int32, (B, B), 0)
    query = lax.broadcasted_iota(jnp.int32, (B, B), 1)
    allowed = key <= query
    for h in range(heads):
        cols = head_columns(h)
        logits = dot(k_ref[:, cols], q_ref[:, cols], ((1,), (1,))) * E**-0.5
        logits = jnp.where(allowed, logits, MASKED)
        top = jnp.max(logits, axis=0, keepdims=True)
        weight_ref[h] = jnp.exp(logits - top)
        gp_ref[h] = dot(v_ref[:, cols], g_ref[:, cols], ((1,), (1,)))
        top_ref[h : h + 1, :] = top


def with_summary(block, summary_ref, which, cols, padded):
    pairs = summary_ref.shape[2]
    parts = [summary_ref[i, which, :, cols].astype(F32) for i in range(2)]
    if padded > 2 * pairs:
        parts.append(jnp.zeros((padded - 2 * pairs, E), F32))
    return jnp.concatenate([block, jnp.concatenate(parts, axis=0).astype(BF16)], axis=0)


def cross_weights_kernel(heads, padded, place_ref, q_ref, k_ref, summary_ref, weight_ref, sums_ref):
    place = place_ref[0]
    pairs = summary_ref.shape[2]
    key = lax.broadcasted_iota(jnp.int32, (B + padded, B), 0)
    query = lax.broadcasted_iota(jnp.int32, (B + padded, B), 1)
    same, other = key - B, key - B - pairs
    pair = lax.shift_right_logical(place, 1)
    allowed = (key < B) & ((key > query) | (key == B - 1))
    allowed |= (same >= 1) & (same < pairs) & (same <= pair)
    allowed |= (other >= 1 - (place & 1)) & (other < pairs) & (other <= pair)
    for h in range(heads):
        cols = head_columns(h)
        k = with_summary(k_ref[:, cols], summary_ref, 0, cols, padded)
        logits = jnp.where(allowed, dot(k, q_ref[:, cols], ((1,), (1,))) * E**-0.5, MASKED)
        top = jnp.max(logits, axis=0, keepdims=True)
        weight = jnp.exp(logits - top)
        weight_ref[h] = weight
        sums_ref[h : h + 1, :] = top
        sums_ref[heads + h : heads + h + 1, :] = jnp.sum(weight, axis=0, keepdims=True)


def cross_scores_kernel(
    heads, padded, q_ref, g_ref, v_ref, summary_ref, weight_ref, sums_ref,
    low_ref, grads_ref, stats_ref, same_ref, other_ref
):
    pairs = summary_ref.shape[2]
    scale = E**-0.5
    for h in range(heads):
        cols = head_columns(h)
        v = with_summary(v_ref[:, cols], summary_ref, 1, cols, padded)
        grad_probs = dot(v, g_ref[:B, cols], ((1,), (1,)))
        own_log, own_inner = stats_of(g_ref[B:, cols])
        cross_top = sums_ref[h : h + 1, :]
        weight = weight_ref[h]
        top = jnp.maximum(cross_top, own_log)
        own_weight = jnp.exp(own_log - top)
        cross_weight = jnp.exp(cross_top - top)
        total = own_weight + cross_weight * sums_ref[heads + h : heads + h + 1, :]
        own_part = own_weight / total
        cross_part = cross_weight / total
        inner = own_part * own_inner + cross_part * jnp.sum(
            weight * grad_probs, axis=0, keepdims=True
        )
        probs = weight * cross_part
        low_ref[h] = probs.astype(BF16)
        grads_ref[h] = (probs * (grad_probs - inner)).astype(BF16)
        stats_ref[:, cols] = stat_rows(top + jnp.log(total), inner)
    for h in range(heads):
        cols = head_columns(h)
        grad_k = scale * dot(grads_ref[h, B:, :], q_ref[:, cols], ((1,), (0,)))
        grad_v = dot(low_ref[h, B:, :], g_ref[:B, cols], ((1,), (0,)))
        for i, grad in enumerate((grad_k, grad_v)):
            same_ref[i, :, cols] = grad[:pairs]
            other_ref[i, :, cols] = grad[pairs : 2 * pairs]


def cross_queries_kernel(heads, padded, k_ref, summary_ref, grads_ref, stats_ref, gq_ref):
    gq_ref[B:, :] = stats_ref[...]
    for h in range(heads):
        cols = head_columns(h)
        k = with_summary(k_ref[:, cols], summary_ref, 0, cols, padded)
        gq_ref[:B, cols] = (E**-0.5 * dot(grads_ref[h], k, ((0,), (0,)))).astype(BF16)


def cross_keys_kernel(heads, q_ref, g_ref, low_ref, grads_ref, gk_ref, gv_ref):
    for h in range(heads):
        cols = head_columns(h)
        gk_ref[:, cols] = E**-0.5 * dot(grads_ref[h, :B, :], q_ref[:, cols], ((1,), (0,)))
        gv_ref[:, cols] = dot(low_ref[h, :B, :], g_ref[:B, cols], ((1,), (0,)))


def final_kernel(
    heads, place_ref, q_ref, g_ref, k_ref, own_ref, weight_ref, gp_ref, top_ref, back_ref,
    gk_ref, gv_ref, gs_ref, out_q_ref, out_k_ref, out_v_ref,
    low, grads, done_q, done_k, done_v, sems
):
    first = place_ref[0] == 0
    scale = E**-0.5
    group = heads // 4 if heads % 4 == 0 else heads
    last_row = lax.broadcasted_iota(jnp.int32, (B, B), 0) == B - 1
    for h in range(heads):
        cols = head_columns(h)
        log_total, inner = stats_of(jnp.where(first, own_ref[:, cols], back_ref[B:, cols]))
        probs = weight_ref[h] * jnp.exp(top_ref[h : h + 1, :] - log_total)
        low[h] = probs.astype(BF16)
        grads[h] = (probs * (gp_ref[h] - inner)).astype(BF16)

    copies = []
    for h in range(heads):
        cols = head_columns(h)
        grad_logits = grads[h]
        grad_q = scale * dot(grad_logits, k_ref[:, cols], ((0,), (0,)))
        grad_k = scale * dot(grad_logits, q_ref[:, cols], ((1,), (0,)))
        grad_v = dot(low[h], g_ref[:, cols], ((1,), (0,)))
        grad_k += gk_ref[:, cols] + jnp.where(last_row, gs_ref[0, :, cols], 0.0)
        grad_v += gv_ref[:, cols] + jnp.where(last_row, gs_ref[1, :, cols], 0.0)
        done_q[:, cols] = (grad_q + back_ref[:B, cols].astype(F32)).astype(BF16)
        done_k[:, cols] = grad_k.astype(BF16)
        done_v[:, cols] = grad_v.astype(BF16)
        if (h + 1) % group == 0:
            part = slice((h + 1 - group) * E, (h + 1) * E)
            for done, out in (done_q, out_q_ref), (done_k, out_k_ref), (done_v, out_v_ref):
                copies.append(
                    pltpu.make_async_copy(
                        done.at[:, part], out.at[:, part], sems.at[len(copies)]
                    )
                )
                copies[-1].start()
    for copy in copies:
        copy.wait()


def body(queries, key_vectors, value_vectors, grad_out):
    shard_len, features = queries.shape
    count = lax.axis_size("seq")
    assert shard_len == B and count % 2 == 0
    heads = features // E
    place = lax.axis_index("seq").astype(jnp.int32).reshape(1)
    vmem = pl.BlockSpec(memory_space=pltpu.VMEM)
    smem = pl.BlockSpec(memory_space=pltpu.SMEM)
    anywhere = pl.BlockSpec(memory_space=pl.ANY)

    def kernel(
        function,
        name,
        products,
        inputs,
        outputs,
        spec=vmem,
        scratch=(),
        scalar=False,
        source=vmem,
        limit=16 << 20,
    ):
        out_shape = [jax.ShapeDtypeStruct(shape, kind) for shape, kind in outputs]
        moved = sum(x.size * x.dtype.itemsize for x in (*inputs, *out_shape))
        return pl.pallas_call(
            function,
            in_specs=[smem] * scalar + [source] * (len(inputs) - scalar),
            out_specs=[spec] * len(out_shape),
            out_shape=out_shape,
            scratch_shapes=scratch,
            compiler_params=pltpu.CompilerParams(vmem_limit_bytes=limit),
            cost_estimate=pl.CostEstimate(
                flops=products * 2 * heads * B * B * E,
                bytes_accessed=moved,
                transcendentals=heads * B * B,
            ),
            name=name,
        )(*inputs)

    rows = jnp.stack([key_vectors[B - 1 :], value_vectors[B - 1 :]])
    across = [(i, i ^ 1) for i in range(count)]
    swap = lax.ppermute(rows, "seq", across)
    rows, queries = lax.optimization_barrier((rows, queries))
    next_q = passed_round(queries, -1)
    summary = jnp.stack([rows, swap])
    while 2 * summary.shape[2] < count:
        earlier = passed_along(summary, 2 * summary.shape[2])
        summary = jnp.concatenate([summary, earlier], axis=2)
    pairs = summary.shape[2]
    padded = -(-2 * pairs // 16) * 16
    _, grad_out = lax.optimization_barrier((swap, grad_out))
    grad_stats, own_stats = kernel(
        functools.partial(own_kernel, heads),
        "own",
        2,
        (queries, key_vectors, value_vectors, grad_out),
        [
            ((B + STAT_ROWS, features), BF16),
            ((STAT_ROWS, features), BF16),
        ],
        source=anywhere,
        limit=None,
        scratch=[pltpu.VMEM((B, features), BF16)] * 4 + [pltpu.SemaphoreType.DMA((16,))],
    )

    next_g = passed_along(grad_stats, -1)
    grad_out, next_q = lax.optimization_barrier((grad_out, next_q))
    weight, grad_probs, top = kernel(
        functools.partial(own_weights_kernel, heads),
        "own_weights",
        2,
        (queries, key_vectors, value_vectors, grad_out),
        [((heads, B, B), F32)] * 2 + [((heads, B), F32)],
    )

    wide = heads, B + padded, B
    cross_weight, cross_sums = kernel(
        functools.partial(cross_weights_kernel, heads, padded),
        "cross_weights",
        1,
        (place, next_q, key_vectors, summary),
        [(wide, F32), ((2 * heads, B), F32)],
        scalar=True,
    )
    low, grads, stats, same, other = kernel(
        functools.partial(cross_scores_kernel, heads, padded),
        "cross_scores",
        2,
        (next_q, next_g, value_vectors, summary, cross_weight, cross_sums),
        [
            (wide, BF16),
            (wide, BF16),
            ((STAT_ROWS, features), BF16),
            ((2, pairs, features), F32),
            ((2, pairs, features), F32),
        ],
    )
    other = lax.ppermute(other, "seq", across)
    (grad_q_next,) = kernel(
        functools.partial(cross_queries_kernel, heads, padded),
        "cross_queries",
        1,
        (key_vectors, summary, grads, stats),
        [((B + STAT_ROWS, features), BF16)],
    )
    back = passed_along(grad_q_next, 1)
    grad_k, grad_v = kernel(
        functools.partial(cross_keys_kernel, heads),
        "cross_keys",
        2,
        (next_q, next_g, low, grads),
        [((B, features), F32)] * 2,
    )
    grad_summary = same + other
    while pairs > 1:
        ways = 4 if pairs % 4 == 0 else 2
        pairs //= ways
        parts = [grad_summary[:, i * pairs : (i + 1) * pairs] for i in range(ways)]
        sent = [passed_along(parts[i], -2 * pairs * i) for i in range(1, ways)]
        grad_summary = sum(sent, parts[0])

    return kernel(
        functools.partial(final_kernel, heads),
        "final",
        3,
        (
            place,
            queries,
            grad_out,
            key_vectors,
            own_stats,
            weight,
            grad_probs,
            top,
            back,
            grad_k,
            grad_v,
            grad_summary,
        ),
        [((B, features), BF16)] * 3,
        spec=anywhere,
        scratch=[
            pltpu.VMEM((heads, B, B), BF16),
            pltpu.VMEM((heads, B, B), BF16),
            pltpu.VMEM((B, features), BF16),
            pltpu.VMEM((B, features), BF16),
            pltpu.VMEM((B, features), BF16),
            pltpu.SemaphoreType.DMA((12,)),
        ],
        scalar=True,
    )


def solution(mesh):
    spec = P(("dp", "seq"), "head")
    return jax.shard_map(
        body,
        mesh=mesh,
        in_specs=(spec,) * 4,
        out_specs=(spec,) * 3,
        check_vma=False,
    )
```

```python
import functools

import jax
import jax.numpy as jnp
from jax import lax
from jax.experimental import pallas as pl
from jax.experimental.pallas import tpu as pltpu
from jax.sharding import PartitionSpec as P

E = 128
B = 128
STAT_ROWS = 8
MASKED = -1e30
F32 = jnp.float32
BF16 = jnp.bfloat16


def dot(a, b, contract):
    return lax.dot_general(a, b, (contract, ((), ())), preferred_element_type=F32)


def passed_along(block, distance):
    count = lax.axis_size("seq")
    route = [(i - distance, i) for i in range(count) if 0 <= i - distance < count]
    return lax.ppermute(block, "seq", route)


def passed_round(block, distance):
    count = lax.axis_size("seq")
    return lax.ppermute(block, "seq", [(i, (i + distance) % count) for i in range(count)])


def in_three(x):
    high = x.astype(BF16).astype(F32)
    middle = (x - high).astype(BF16).astype(F32)
    low = (x - high - middle).astype(BF16).astype(F32)
    return [high, middle, low]


def stat_rows(log_total, inner):
    rows = in_three(log_total) + in_three(inner)
    rows.append(jnp.zeros((STAT_ROWS - len(rows), E), F32))
    return jnp.concatenate(rows, axis=0).astype(BF16)


def stats_of(rows):
    rows = rows.astype(F32)
    return rows[0:1] + rows[1:2] + rows[2:3], rows[3:4] + rows[4:5] + rows[5:6]


def head_columns(head):
    return slice(head * E, (head + 1) * E)


def own_kernel(
    heads, q_hbm, k_hbm, v_hbm, g_hbm, out_ref, stats_ref, q_ref, k_ref, v_ref, g_ref, sems
):
    group = heads // 4 if heads % 4 == 0 else heads
    pairs = (q_hbm, q_ref), (k_hbm, k_ref), (v_hbm, v_ref), (g_hbm, g_ref)
    copies = []
    for start in range(0, heads, group):
        part = slice(start * E, (start + group) * E)
        for source, target in pairs:
            copies.append(
                pltpu.make_async_copy(
                    source.at[:, part], target.at[:, part], sems.at[len(copies)]
                )
            )
            copies[-1].start()
    key = lax.broadcasted_iota(jnp.int32, (B, B), 0)
    query = lax.broadcasted_iota(jnp.int32, (B, B), 1)
    allowed = key <= query
    for h in range(heads):
        if h % group == 0:
            for copy in copies[h // group * 4 : h // group * 4 + 4]:
                copy.wait()
        cols = head_columns(h)
        q, k, v, g = q_ref[:, cols], k_ref[:, cols], v_ref[:, cols], g_ref[:, cols]
        logits = jnp.where(allowed, dot(k, q, ((1,), (1,))) * E**-0.5, MASKED)
        top = jnp.max(logits, axis=0, keepdims=True)
        weight = jnp.exp(logits - top)
        grad_probs = dot(v, g, ((1,), (1,)))
        total = jnp.sum(weight, axis=0, keepdims=True)
        inner = jnp.sum(weight * grad_probs, axis=0, keepdims=True)
        out_ref[:B, cols] = g
        stats = stat_rows(top + jnp.log(total), inner / total)
        out_ref[B:, cols] = stats
        stats_ref[:, cols] = stats


def own_weights_kernel(heads, q_ref, k_ref, v_ref, g_ref, weight_ref, gp_ref, top_ref):
    key = lax.broadcasted_iota(jnp.int32, (B, B), 0)
    query = lax.broadcasted_iota(jnp.int32, (B, B), 1)
    allowed = key <= query
    for h in range(heads):
        cols = head_columns(h)
        logits = dot(k_ref[:, cols], q_ref[:, cols], ((1,), (1,))) * E**-0.5
        logits = jnp.where(allowed, logits, MASKED)
        top = jnp.max(logits, axis=0, keepdims=True)
        weight_ref[h] = jnp.exp(logits - top)
        gp_ref[h] = dot(v_ref[:, cols], g_ref[:, cols], ((1,), (1,)))
        top_ref[h : h + 1, :] = top


def with_summary(block, summary_ref, which, cols, padded):
    pairs = summary_ref.shape[2]
    parts = [summary_ref[i, which, :, cols].astype(F32) for i in range(2)]
    if padded > 2 * pairs:
        parts.append(jnp.zeros((padded - 2 * pairs, E), F32))
    return jnp.concatenate([block, jnp.concatenate(parts, axis=0).astype(BF16)], axis=0)


def cross_weights_kernel(heads, padded, place_ref, q_ref, k_ref, summary_ref, weight_ref, sums_ref):
    place = place_ref[0]
    pairs = summary_ref.shape[2]
    key = lax.broadcasted_iota(jnp.int32, (B + padded, B), 0)
    query = lax.broadcasted_iota(jnp.int32, (B + padded, B), 1)
    same, other = key - B, key - B - pairs
    pair = lax.shift_right_logical(place, 1)
    allowed = (key < B) & ((key > query) | (key == B - 1))
    allowed |= (same >= 1) & (same < pairs) & (same <= pair)
    allowed |= (other >= 1 - (place & 1)) & (other < pairs) & (other <= pair)
    for h in range(heads):
        cols = head_columns(h)
        k = with_summary(k_ref[:, cols], summary_ref, 0, cols, padded)
        logits = jnp.where(allowed, dot(k, q_ref[:, cols], ((1,), (1,))) * E**-0.5, MASKED)
        top = jnp.max(logits, axis=0, keepdims=True)
        weight = jnp.exp(logits - top)
        weight_ref[h] = weight
        sums_ref[h : h + 1, :] = top
        sums_ref[heads + h : heads + h + 1, :] = jnp.sum(weight, axis=0, keepdims=True)


def cross_scores_kernel(
    heads, padded, q_ref, g_ref, v_ref, summary_ref, weight_ref, sums_ref,
    low_ref, grads_ref, stats_ref, same_ref, other_ref
):
    pairs = summary_ref.shape[2]
    scale = E**-0.5
    for h in range(heads):
        cols = head_columns(h)
        v = with_summary(v_ref[:, cols], summary_ref, 1, cols, padded)
        grad_probs = dot(v, g_ref[:B, cols], ((1,), (1,)))
        own_log, own_inner = stats_of(g_ref[B:, cols])
        cross_top = sums_ref[h : h + 1, :]
        weight = weight_ref[h]
        top = jnp.maximum(cross_top, own_log)
        own_weight = jnp.exp(own_log - top)
        cross_weight = jnp.exp(cross_top - top)
        total = own_weight + cross_weight * sums_ref[heads + h : heads + h + 1, :]
        own_part = own_weight / total
        cross_part = cross_weight / total
        inner = own_part * own_inner + cross_part * jnp.sum(
            weight * grad_probs, axis=0, keepdims=True
        )
        probs = weight * cross_part
        low_ref[h] = probs.astype(BF16)
        grads_ref[h] = (probs * (grad_probs - inner)).astype(BF16)
        stats_ref[:, cols] = stat_rows(top + jnp.log(total), inner)
    for h in range(heads):
        cols = head_columns(h)
        grad_k = scale * dot(grads_ref[h, B:, :], q_ref[:, cols], ((1,), (0,)))
        grad_v = dot(low_ref[h, B:, :], g_ref[:B, cols], ((1,), (0,)))
        for i, grad in enumerate((grad_k, grad_v)):
            same_ref[i, :, cols] = grad[:pairs]
            other_ref[i, :, cols] = grad[pairs : 2 * pairs].astype(BF16)


def cross_queries_kernel(heads, padded, k_ref, summary_ref, grads_ref, stats_ref, gq_ref):
    gq_ref[B:, :] = stats_ref[...]
    for h in range(heads):
        cols = head_columns(h)
        k = with_summary(k_ref[:, cols], summary_ref, 0, cols, padded)
        gq_ref[:B, cols] = (E**-0.5 * dot(grads_ref[h], k, ((0,), (0,)))).astype(BF16)


def cross_keys_kernel(heads, q_ref, g_ref, low_ref, grads_ref, gk_ref, gv_ref):
    for h in range(heads):
        cols = head_columns(h)
        gk_ref[:, cols] = E**-0.5 * dot(grads_ref[h, :B, :], q_ref[:, cols], ((1,), (0,)))
        gv_ref[:, cols] = dot(low_ref[h, :B, :], g_ref[:B, cols], ((1,), (0,)))


def final_kernel(
    heads, place_ref, q_ref, g_ref, k_ref, own_ref, weight_ref, gp_ref, top_ref, back_ref,
    gk_ref, gv_ref, gs_ref, out_q_ref, out_k_ref, out_v_ref,
    low, grads, done_q, done_k, done_v, sems
):
    first = place_ref[0] == 0
    scale = E**-0.5
    group = heads // 4 if heads % 4 == 0 else heads
    last_row = lax.broadcasted_iota(jnp.int32, (B, B), 0) == B - 1
    for h in range(heads):
        cols = head_columns(h)
        log_total, inner = stats_of(jnp.where(first, own_ref[:, cols], back_ref[B:, cols]))
        probs = weight_ref[h] * jnp.exp(top_ref[h : h + 1, :] - log_total)
        low[h] = probs.astype(BF16)
        grads[h] = (probs * (gp_ref[h] - inner)).astype(BF16)

    copies = []

    def put(done, out, h):
        if (h + 1) % group == 0:
            part = slice((h + 1 - group) * E, (h + 1) * E)
            sem = sems.at[len(copies)]
            copies.append(pltpu.make_async_copy(done.at[:, part], out.at[:, part], sem))
            copies[-1].start()

    for h in range(heads):
        cols = head_columns(h)
        grad_q = scale * dot(grads[h], k_ref[:, cols], ((0,), (0,)))
        done_q[:, cols] = (grad_q + back_ref[:B, cols].astype(F32)).astype(BF16)
        put(done_q, out_q_ref, h)
    for h in range(heads):
        cols = head_columns(h)
        grad_k = scale * dot(grads[h], q_ref[:, cols], ((1,), (0,)))
        grad_k += gk_ref[:, cols] + jnp.where(last_row, gs_ref[0, :, cols], 0.0)
        done_k[:, cols] = grad_k.astype(BF16)
        put(done_k, out_k_ref, h)
    for h in range(heads):
        cols = head_columns(h)
        grad_v = dot(low[h], g_ref[:, cols], ((1,), (0,)))
        grad_v += gv_ref[:, cols] + jnp.where(last_row, gs_ref[1, :, cols], 0.0)
        done_v[:, cols] = grad_v.astype(BF16)
        put(done_v, out_v_ref, h)
    for copy in copies:
        copy.wait()


def body(queries, key_vectors, value_vectors, grad_out):
    shard_len, features = queries.shape
    count = lax.axis_size("seq")
    assert shard_len == B and count % 2 == 0
    heads = features // E
    place = lax.axis_index("seq").astype(jnp.int32).reshape(1)
    vmem = pl.BlockSpec(memory_space=pltpu.VMEM)
    smem = pl.BlockSpec(memory_space=pltpu.SMEM)
    anywhere = pl.BlockSpec(memory_space=pl.ANY)

    def kernel(
        function,
        name,
        products,
        inputs,
        outputs,
        spec=vmem,
        scratch=(),
        scalar=False,
        source=vmem,
        limit=16 << 20,
    ):
        out_shape = [jax.ShapeDtypeStruct(shape, kind) for shape, kind in outputs]
        moved = sum(x.size * x.dtype.itemsize for x in (*inputs, *out_shape))
        return pl.pallas_call(
            function,
            in_specs=[smem] * scalar + [source] * (len(inputs) - scalar),
            out_specs=[spec] * len(out_shape),
            out_shape=out_shape,
            scratch_shapes=scratch,
            compiler_params=pltpu.CompilerParams(vmem_limit_bytes=limit),
            cost_estimate=pl.CostEstimate(
                flops=products * 2 * heads * B * B * E,
                bytes_accessed=moved,
                transcendentals=heads * B * B,
            ),
            name=name,
        )(*inputs)

    rows = jnp.stack([key_vectors[B - 1 :], value_vectors[B - 1 :]])
    across = [(i, i ^ 1) for i in range(count)]
    swap = lax.ppermute(rows, "seq", across)
    rows, queries = lax.optimization_barrier((rows, queries))
    next_q = passed_round(queries, -1)
    summary = jnp.stack([rows, swap])
    while 2 * summary.shape[2] < count:
        earlier = passed_along(summary, 2 * summary.shape[2])
        summary = jnp.concatenate([summary, earlier], axis=2)
    pairs = summary.shape[2]
    padded = -(-2 * pairs // 16) * 16
    _, grad_out = lax.optimization_barrier((swap, grad_out))
    grad_stats, own_stats = kernel(
        functools.partial(own_kernel, heads),
        "own",
        2,
        (queries, key_vectors, value_vectors, grad_out),
        [
            ((B + STAT_ROWS, features), BF16),
            ((STAT_ROWS, features), BF16),
        ],
        source=anywhere,
        limit=None,
        scratch=[pltpu.VMEM((B, features), BF16)] * 4 + [pltpu.SemaphoreType.DMA((16,))],
    )

    next_g = passed_along(grad_stats, -1)
    grad_out, next_q = lax.optimization_barrier((grad_out, next_q))
    weight, grad_probs, top = kernel(
        functools.partial(own_weights_kernel, heads),
        "own_weights",
        2,
        (queries, key_vectors, value_vectors, grad_out),
        [((heads, B, B), F32)] * 2 + [((heads, B), F32)],
    )

    wide = heads, B + padded, B
    cross_weight, cross_sums = kernel(
        functools.partial(cross_weights_kernel, heads, padded),
        "cross_weights",
        1,
        (place, next_q, key_vectors, summary),
        [(wide, F32), ((2 * heads, B), F32)],
        scalar=True,
    )
    low, grads, stats, same, other = kernel(
        functools.partial(cross_scores_kernel, heads, padded),
        "cross_scores",
        2,
        (next_q, next_g, value_vectors, summary, cross_weight, cross_sums),
        [
            (wide, BF16),
            (wide, BF16),
            ((STAT_ROWS, features), BF16),
            ((2, pairs, features), F32),
            ((2, pairs, features), BF16),
        ],
    )
    other = lax.ppermute(other, "seq", across)
    (grad_q_next,) = kernel(
        functools.partial(cross_queries_kernel, heads, padded),
        "cross_queries",
        1,
        (key_vectors, summary, grads, stats),
        [((B + STAT_ROWS, features), BF16)],
    )
    back = passed_along(grad_q_next, 1)
    grad_k, grad_v = kernel(
        functools.partial(cross_keys_kernel, heads),
        "cross_keys",
        2,
        (next_q, next_g, low, grads),
        [((B, features), F32)] * 2,
    )
    grad_summary = same + other.astype(F32)
    while pairs > 1:
        ways = 4 if pairs % 4 == 0 else 2
        pairs //= ways
        parts = [grad_summary[:, i * pairs : (i + 1) * pairs] for i in range(ways)]
        sent = [passed_along(parts[i], -2 * pairs * i) for i in range(1, ways)]
        grad_summary = sum(sent, parts[0])

    return kernel(
        functools.partial(final_kernel, heads),
        "final",
        3,
        (
            place,
            queries,
            grad_out,
            key_vectors,
            own_stats,
            weight,
            grad_probs,
            top,
            back,
            grad_k,
            grad_v,
            grad_summary,
        ),
        [((B, features), BF16)] * 3,
        spec=anywhere,
        scratch=[
            pltpu.VMEM((heads, B, B), BF16),
            pltpu.VMEM((heads, B, B), BF16),
            pltpu.VMEM((B, features), BF16),
            pltpu.VMEM((B, features), BF16),
            pltpu.VMEM((B, features), BF16),
            pltpu.SemaphoreType.DMA((12,)),
        ],
        scalar=True,
    )


def solution(mesh):
    spec = P(("dp", "seq"), "head")
    return jax.shard_map(
        body,
        mesh=mesh,
        in_specs=(spec,) * 4,
        out_specs=(spec,) * 3,
        check_vma=False,
    )
```

```python
import functools

import jax
import jax.numpy as jnp
from jax import lax
from jax.experimental import pallas as pl
from jax.experimental.pallas import tpu as pltpu
from jax.sharding import PartitionSpec as P

E = 128
B = 128
STAT_ROWS = 8
MASKED = -1e30
F32 = jnp.float32
BF16 = jnp.bfloat16


def dot(a, b, contract):
    return lax.dot_general(a, b, (contract, ((), ())), preferred_element_type=F32)


def passed_along(block, distance):
    count = lax.axis_size("seq")
    route = [(i - distance, i) for i in range(count) if 0 <= i - distance < count]
    return lax.ppermute(block, "seq", route)


def passed_round(block, distance):
    count = lax.axis_size("seq")
    return lax.ppermute(block, "seq", [(i, (i + distance) % count) for i in range(count)])


def in_three(x):
    high = x.astype(BF16).astype(F32)
    middle = (x - high).astype(BF16).astype(F32)
    low = (x - high - middle).astype(BF16).astype(F32)
    return [high, middle, low]


def stat_rows(log_total, inner):
    rows = in_three(log_total) + in_three(inner)
    rows.append(jnp.zeros((STAT_ROWS - len(rows), E), F32))
    return jnp.concatenate(rows, axis=0).astype(BF16)


def stats_of(rows):
    rows = rows.astype(F32)
    return rows[0:1] + rows[1:2] + rows[2:3], rows[3:4] + rows[4:5] + rows[5:6]


def head_columns(head):
    return slice(head * E, (head + 1) * E)


def own_kernel(
    heads, q_hbm, k_hbm, v_hbm, g_hbm, out_ref, stats_ref, q_ref, k_ref, v_ref, g_ref, sems
):
    group = heads // 4 if heads % 4 == 0 else heads
    pairs = (q_hbm, q_ref), (k_hbm, k_ref), (v_hbm, v_ref), (g_hbm, g_ref)
    copies = []
    for start in range(0, heads, group):
        part = slice(start * E, (start + group) * E)
        for source, target in pairs:
            copies.append(
                pltpu.make_async_copy(
                    source.at[:, part], target.at[:, part], sems.at[len(copies)]
                )
            )
            copies[-1].start()
    key = lax.broadcasted_iota(jnp.int32, (B, B), 0)
    query = lax.broadcasted_iota(jnp.int32, (B, B), 1)
    allowed = key <= query
    for h in range(heads):
        if h % group == 0:
            for copy in copies[h // group * 4 : h // group * 4 + 4]:
                copy.wait()
        cols = head_columns(h)
        q, k, v, g = q_ref[:, cols], k_ref[:, cols], v_ref[:, cols], g_ref[:, cols]
        logits = jnp.where(allowed, dot(k, q, ((1,), (1,))) * E**-0.5, MASKED)
        top = jnp.max(logits, axis=0, keepdims=True)
        weight = jnp.exp(logits - top)
        grad_probs = dot(v, g, ((1,), (1,)))
        total = jnp.sum(weight, axis=0, keepdims=True)
        inner = jnp.sum(weight * grad_probs, axis=0, keepdims=True)
        out_ref[:B, cols] = g
        stats = stat_rows(top + jnp.log(total), inner / total)
        out_ref[B:, cols] = stats
        stats_ref[:, cols] = stats


def own_weights_kernel(heads, q_ref, k_ref, v_ref, g_ref, weight_ref, gp_ref, top_ref):
    key = lax.broadcasted_iota(jnp.int32, (B, B), 0)
    query = lax.broadcasted_iota(jnp.int32, (B, B), 1)
    allowed = key <= query
    for h in range(heads):
        cols = head_columns(h)
        logits = dot(k_ref[:, cols], q_ref[:, cols], ((1,), (1,))) * E**-0.5
        logits = jnp.where(allowed, logits, MASKED)
        top = jnp.max(logits, axis=0, keepdims=True)
        weight_ref[h] = jnp.exp(logits - top)
        gp_ref[h] = dot(v_ref[:, cols], g_ref[:, cols], ((1,), (1,)))
        top_ref[h : h + 1, :] = top


def with_summary(block, summary_ref, which, cols, padded):
    pairs = summary_ref.shape[2]
    parts = [summary_ref[i, which, :, cols].astype(F32) for i in range(2)]
    if padded > 2 * pairs:
        parts.append(jnp.zeros((padded - 2 * pairs, E), F32))
    return jnp.concatenate([block, jnp.concatenate(parts, axis=0).astype(BF16)], axis=0)


def cross_weights_kernel(heads, padded, place_ref, q_ref, k_ref, summary_ref, weight_ref, sums_ref):
    place = place_ref[0]
    pairs = summary_ref.shape[2]
    key = lax.broadcasted_iota(jnp.int32, (B + padded, B), 0)
    query = lax.broadcasted_iota(jnp.int32, (B + padded, B), 1)
    same, other = key - B, key - B - pairs
    pair = lax.shift_right_logical(place, 1)
    allowed = (key < B) & ((key > query) | (key == B - 1))
    allowed |= (same >= 1) & (same < pairs) & (same <= pair)
    allowed |= (other >= 1 - (place & 1)) & (other < pairs) & (other <= pair)
    for h in range(heads):
        cols = head_columns(h)
        k = with_summary(k_ref[:, cols], summary_ref, 0, cols, padded)
        logits = jnp.where(allowed, dot(k, q_ref[:, cols], ((1,), (1,))) * E**-0.5, MASKED)
        top = jnp.max(logits, axis=0, keepdims=True)
        weight = jnp.exp(logits - top)
        weight_ref[h] = weight
        sums_ref[h : h + 1, :] = top
        sums_ref[heads + h : heads + h + 1, :] = jnp.sum(weight, axis=0, keepdims=True)


def cross_scores_kernel(
    heads, padded, q_ref, g_ref, k_ref, v_ref, summary_ref, weight_ref, sums_ref,
    low_ref, grads_ref, same_ref, other_ref, gq_ref
):
    pairs = summary_ref.shape[2]
    scale = E**-0.5
    for h in range(heads):
        cols = head_columns(h)
        v = with_summary(v_ref[:, cols], summary_ref, 1, cols, padded)
        grad_probs = dot(v, g_ref[:B, cols], ((1,), (1,)))
        own_log, own_inner = stats_of(g_ref[B:, cols])
        cross_top = sums_ref[h : h + 1, :]
        weight = weight_ref[h]
        top = jnp.maximum(cross_top, own_log)
        own_weight = jnp.exp(own_log - top)
        cross_weight = jnp.exp(cross_top - top)
        total = own_weight + cross_weight * sums_ref[heads + h : heads + h + 1, :]
        own_part = own_weight / total
        cross_part = cross_weight / total
        inner = own_part * own_inner + cross_part * jnp.sum(
            weight * grad_probs, axis=0, keepdims=True
        )
        probs = weight * cross_part
        low_ref[h] = probs.astype(BF16)
        grads_ref[h] = (probs * (grad_probs - inner)).astype(BF16)
        gq_ref[B:, cols] = stat_rows(top + jnp.log(total), inner)
    for h in range(heads):
        cols = head_columns(h)
        grad_k = scale * dot(grads_ref[h, B:, :], q_ref[:, cols], ((1,), (0,)))
        grad_v = dot(low_ref[h, B:, :], g_ref[:B, cols], ((1,), (0,)))
        for i, grad in enumerate((grad_k, grad_v)):
            same_ref[i, :, cols] = grad[:pairs]
            other_ref[i, :, cols] = grad[pairs : 2 * pairs].astype(BF16)
    for h in range(heads):
        cols = head_columns(h)
        k = with_summary(k_ref[:, cols], summary_ref, 0, cols, padded)
        gq_ref[:B, cols] = (scale * dot(grads_ref[h], k, ((0,), (0,)))).astype(BF16)


def cross_keys_kernel(heads, q_ref, g_ref, low_ref, grads_ref, gk_ref, gv_ref):
    for h in range(heads):
        cols = head_columns(h)
        gk_ref[:, cols] = E**-0.5 * dot(grads_ref[h, :B, :], q_ref[:, cols], ((1,), (0,)))
        gv_ref[:, cols] = dot(low_ref[h, :B, :], g_ref[:B, cols], ((1,), (0,)))


def final_kernel(
    heads, place_ref, q_ref, g_ref, k_ref, own_ref, weight_ref, gp_ref, top_ref, back_ref,
    gk_ref, gv_ref, gs_ref, out_q_ref, out_k_ref, out_v_ref,
    low, grads, done_q, done_k, done_v, sems
):
    first = place_ref[0] == 0
    scale = E**-0.5
    group = heads // 4 if heads % 4 == 0 else heads
    last_row = lax.broadcasted_iota(jnp.int32, (B, B), 0) == B - 1
    for h in range(heads):
        cols = head_columns(h)
        log_total, inner = stats_of(jnp.where(first, own_ref[:, cols], back_ref[B:, cols]))
        probs = weight_ref[h] * jnp.exp(top_ref[h : h + 1, :] - log_total)
        low[h] = probs.astype(BF16)
        grads[h] = (probs * (gp_ref[h] - inner)).astype(BF16)

    copies = []

    def put(done, out, h):
        if (h + 1) % group == 0:
            part = slice((h + 1 - group) * E, (h + 1) * E)
            sem = sems.at[len(copies)]
            copies.append(pltpu.make_async_copy(done.at[:, part], out.at[:, part], sem))
            copies[-1].start()

    for h in range(heads):
        cols = head_columns(h)
        grad_q = scale * dot(grads[h], k_ref[:, cols], ((0,), (0,)))
        done_q[:, cols] = (grad_q + back_ref[:B, cols].astype(F32)).astype(BF16)
        put(done_q, out_q_ref, h)
    for h in range(heads):
        cols = head_columns(h)
        grad_k = scale * dot(grads[h], q_ref[:, cols], ((1,), (0,)))
        grad_k += gk_ref[:, cols] + jnp.where(last_row, gs_ref[0, :, cols], 0.0)
        done_k[:, cols] = grad_k.astype(BF16)
        put(done_k, out_k_ref, h)
    for h in range(heads):
        cols = head_columns(h)
        grad_v = dot(low[h], g_ref[:, cols], ((1,), (0,)))
        grad_v += gv_ref[:, cols] + jnp.where(last_row, gs_ref[1, :, cols], 0.0)
        done_v[:, cols] = grad_v.astype(BF16)
        put(done_v, out_v_ref, h)
    for copy in copies:
        copy.wait()


def body(queries, key_vectors, value_vectors, grad_out):
    shard_len, features = queries.shape
    count = lax.axis_size("seq")
    assert shard_len == B and count % 2 == 0
    heads = features // E
    place = lax.axis_index("seq").astype(jnp.int32).reshape(1)
    vmem = pl.BlockSpec(memory_space=pltpu.VMEM)
    smem = pl.BlockSpec(memory_space=pltpu.SMEM)
    anywhere = pl.BlockSpec(memory_space=pl.ANY)

    def kernel(
        function,
        name,
        products,
        inputs,
        outputs,
        spec=vmem,
        scratch=(),
        scalar=False,
        source=vmem,
        limit=16 << 20,
    ):
        out_shape = [jax.ShapeDtypeStruct(shape, kind) for shape, kind in outputs]
        moved = sum(x.size * x.dtype.itemsize for x in (*inputs, *out_shape))
        return pl.pallas_call(
            function,
            in_specs=[smem] * scalar + [source] * (len(inputs) - scalar),
            out_specs=[spec] * len(out_shape),
            out_shape=out_shape,
            scratch_shapes=scratch,
            compiler_params=pltpu.CompilerParams(vmem_limit_bytes=limit),
            cost_estimate=pl.CostEstimate(
                flops=products * 2 * heads * B * B * E,
                bytes_accessed=moved,
                transcendentals=heads * B * B,
            ),
            name=name,
        )(*inputs)

    rows = jnp.stack([key_vectors[B - 1 :], value_vectors[B - 1 :]])
    across = [(i, i ^ 1) for i in range(count)]
    swap = lax.ppermute(rows, "seq", across)
    rows, queries = lax.optimization_barrier((rows, queries))
    next_q = passed_round(queries, -1)
    summary = jnp.stack([rows, swap])
    while 2 * summary.shape[2] < count:
        earlier = passed_along(summary, 2 * summary.shape[2])
        summary = jnp.concatenate([summary, earlier], axis=2)
    pairs = summary.shape[2]
    padded = -(-2 * pairs // 16) * 16
    _, grad_out = lax.optimization_barrier((swap, grad_out))
    grad_stats, own_stats = kernel(
        functools.partial(own_kernel, heads),
        "own",
        2,
        (queries, key_vectors, value_vectors, grad_out),
        [
            ((B + STAT_ROWS, features), BF16),
            ((STAT_ROWS, features), BF16),
        ],
        source=anywhere,
        limit=None,
        scratch=[pltpu.VMEM((B, features), BF16)] * 4 + [pltpu.SemaphoreType.DMA((16,))],
    )

    next_g = passed_along(grad_stats, -1)
    grad_out, next_q = lax.optimization_barrier((grad_out, next_q))
    weight, grad_probs, top = kernel(
        functools.partial(own_weights_kernel, heads),
        "own_weights",
        2,
        (queries, key_vectors, value_vectors, grad_out),
        [((heads, B, B), F32)] * 2 + [((heads, B), F32)],
    )

    wide = heads, B + padded, B
    cross_weight, cross_sums = kernel(
        functools.partial(cross_weights_kernel, heads, padded),
        "cross_weights",
        1,
        (place, next_q, key_vectors, summary),
        [(wide, F32), ((2 * heads, B), F32)],
        scalar=True,
    )
    low, grads, same, other, grad_q_next = kernel(
        functools.partial(cross_scores_kernel, heads, padded),
        "cross_scores",
        3,
        (next_q, next_g, key_vectors, value_vectors, summary, cross_weight, cross_sums),
        [(wide, BF16)] * 2
        + [((2, pairs, features), F32), ((2, pairs, features), BF16)]
        + [((B + STAT_ROWS, features), BF16)],
    )
    other = lax.ppermute(other, "seq", across)
    back = passed_along(grad_q_next, 1)
    grad_k, grad_v = kernel(
        functools.partial(cross_keys_kernel, heads),
        "cross_keys",
        2,
        (next_q, next_g, low, grads),
        [((B, features), F32)] * 2,
    )
    grad_summary = same + other.astype(F32)
    while pairs > 1:
        ways = 4 if pairs % 4 == 0 else 2
        pairs //= ways
        parts = [grad_summary[:, i * pairs : (i + 1) * pairs] for i in range(ways)]
        sent = [passed_along(parts[i], -2 * pairs * i) for i in range(1, ways)]
        grad_summary = sum(sent, parts[0])

    return kernel(
        functools.partial(final_kernel, heads),
        "final",
        3,
        (
            place,
            queries,
            grad_out,
            key_vectors,
            own_stats,
            weight,
            grad_probs,
            top,
            back,
            grad_k,
            grad_v,
            grad_summary,
        ),
        [((B, features), BF16)] * 3,
        spec=anywhere,
        scratch=[
            pltpu.VMEM((heads, B, B), BF16),
            pltpu.VMEM((heads, B, B), BF16),
            pltpu.VMEM((B, features), BF16),
            pltpu.VMEM((B, features), BF16),
            pltpu.VMEM((B, features), BF16),
            pltpu.SemaphoreType.DMA((12,)),
        ],
        scalar=True,
    )


def solution(mesh):
    spec = P(("dp", "seq"), "head")
    return jax.shard_map(
        body,
        mesh=mesh,
        in_specs=(spec,) * 4,
        out_specs=(spec,) * 3,
        check_vma=False,
    )
```

```python
import functools

import jax
import jax.numpy as jnp
from jax import lax
from jax.experimental import pallas as pl
from jax.experimental.pallas import tpu as pltpu
from jax.sharding import PartitionSpec as P

E = 128
B = 128
STAT_ROWS = 8
MASKED = -1e30
F32 = jnp.float32
BF16 = jnp.bfloat16


def dot(a, b, contract):
    return lax.dot_general(a, b, (contract, ((), ())), preferred_element_type=F32)


def passed_along(block, distance):
    count = lax.axis_size("seq")
    route = [(i - distance, i) for i in range(count) if 0 <= i - distance < count]
    return lax.ppermute(block, "seq", route)


def passed_round(block, distance):
    count = lax.axis_size("seq")
    return lax.ppermute(block, "seq", [(i, (i + distance) % count) for i in range(count)])


def in_three(x):
    high = x.astype(BF16).astype(F32)
    middle = (x - high).astype(BF16).astype(F32)
    low = (x - high - middle).astype(BF16).astype(F32)
    return [high, middle, low]


def stat_rows(log_total, inner):
    rows = in_three(log_total) + in_three(inner)
    rows.append(jnp.zeros((STAT_ROWS - len(rows), E), F32))
    return jnp.concatenate(rows, axis=0).astype(BF16)


def stats_of(rows):
    rows = rows.astype(F32)
    return rows[0:1] + rows[1:2] + rows[2:3], rows[3:4] + rows[4:5] + rows[5:6]


def head_columns(head):
    return slice(head * E, (head + 1) * E)


def own_kernel(
    heads, q_hbm, k_hbm, v_hbm, g_hbm, out_ref, stats_ref, q_ref, k_ref, v_ref, g_ref, sems
):
    group = heads // 4 if heads % 4 == 0 else heads
    pairs = (q_hbm, q_ref), (k_hbm, k_ref), (v_hbm, v_ref), (g_hbm, g_ref)
    copies = []
    for start in range(0, heads, group):
        part = slice(start * E, (start + group) * E)
        for source, target in pairs:
            copies.append(
                pltpu.make_async_copy(
                    source.at[:, part], target.at[:, part], sems.at[len(copies)]
                )
            )
            copies[-1].start()
    key = lax.broadcasted_iota(jnp.int32, (B, B), 0)
    query = lax.broadcasted_iota(jnp.int32, (B, B), 1)
    allowed = key <= query
    for h in range(heads):
        if h % group == 0:
            for copy in copies[h // group * 4 : h // group * 4 + 4]:
                copy.wait()
        cols = head_columns(h)
        q, k, v, g = q_ref[:, cols], k_ref[:, cols], v_ref[:, cols], g_ref[:, cols]
        logits = jnp.where(allowed, dot(k, q, ((1,), (1,))) * E**-0.5, MASKED)
        top = jnp.max(logits, axis=0, keepdims=True)
        weight = jnp.exp(logits - top)
        grad_probs = dot(v, g, ((1,), (1,)))
        total = jnp.sum(weight, axis=0, keepdims=True)
        inner = jnp.sum(weight * grad_probs, axis=0, keepdims=True)
        out_ref[:B, cols] = g
        stats = stat_rows(top + jnp.log(total), inner / total)
        out_ref[B:, cols] = stats
        stats_ref[:, cols] = stats


def own_weights_kernel(heads, q_ref, k_ref, v_ref, g_ref, weight_ref, gp_ref, top_ref):
    key = lax.broadcasted_iota(jnp.int32, (B, B), 0)
    query = lax.broadcasted_iota(jnp.int32, (B, B), 1)
    allowed = key <= query
    for h in range(heads):
        cols = head_columns(h)
        logits = dot(k_ref[:, cols], q_ref[:, cols], ((1,), (1,))) * E**-0.5
        logits = jnp.where(allowed, logits, MASKED)
        top = jnp.max(logits, axis=0, keepdims=True)
        weight_ref[h] = jnp.exp(logits - top)
        gp_ref[h] = dot(v_ref[:, cols], g_ref[:, cols], ((1,), (1,)))
        top_ref[h : h + 1, :] = top


def with_summary(block, summary_ref, which, cols, padded):
    pairs = summary_ref.shape[2]
    parts = [summary_ref[i, which, :, cols].astype(F32) for i in range(2)]
    if padded > 2 * pairs:
        parts.append(jnp.zeros((padded - 2 * pairs, E), F32))
    return jnp.concatenate([block, jnp.concatenate(parts, axis=0).astype(BF16)], axis=0)


def cross_weights_kernel(heads, padded, place_ref, q_ref, k_ref, summary_ref, weight_ref, sums_ref):
    place = place_ref[0]
    pairs = summary_ref.shape[2]
    key = lax.broadcasted_iota(jnp.int32, (B + padded, B), 0)
    query = lax.broadcasted_iota(jnp.int32, (B + padded, B), 1)
    same, other = key - B, key - B - pairs
    pair = lax.shift_right_logical(place, 1)
    allowed = (key < B) & ((key > query) | (key == B - 1))
    allowed |= (same >= 1) & (same < pairs) & (same <= pair)
    allowed |= (other >= 1 - (place & 1)) & (other < pairs) & (other <= pair)
    for h in range(heads):
        cols = head_columns(h)
        k = with_summary(k_ref[:, cols], summary_ref, 0, cols, padded)
        logits = jnp.where(allowed, dot(k, q_ref[:, cols], ((1,), (1,))) * E**-0.5, MASKED)
        top = jnp.max(logits, axis=0, keepdims=True)
        weight = jnp.exp(logits - top)
        weight_ref[h] = weight
        sums_ref[h : h + 1, :] = top
        sums_ref[heads + h : heads + h + 1, :] = jnp.sum(weight, axis=0, keepdims=True)


def cross_scores_kernel(
    heads, padded, q_ref, g_ref, k_ref, v_ref, summary_ref, weight_ref, sums_ref,
    low_ref, grads_ref, same_ref, other_ref, gq_ref
):
    pairs = summary_ref.shape[2]
    scale = E**-0.5
    for h in range(heads):
        cols = head_columns(h)
        v = with_summary(v_ref[:, cols], summary_ref, 1, cols, padded)
        grad_probs = dot(v, g_ref[:B, cols], ((1,), (1,)))
        own_log, own_inner = stats_of(g_ref[B:, cols])
        cross_top = sums_ref[h : h + 1, :]
        weight = weight_ref[h]
        top = jnp.maximum(cross_top, own_log)
        own_weight = jnp.exp(own_log - top)
        cross_weight = jnp.exp(cross_top - top)
        total = own_weight + cross_weight * sums_ref[heads + h : heads + h + 1, :]
        own_part = own_weight / total
        cross_part = cross_weight / total
        inner = own_part * own_inner + cross_part * jnp.sum(
            weight * grad_probs, axis=0, keepdims=True
        )
        probs = weight * cross_part
        low_ref[h] = probs.astype(BF16)
        grads_ref[h] = (probs * (grad_probs - inner)).astype(BF16)
        gq_ref[B:, cols] = stat_rows(top + jnp.log(total), inner)
    for h in range(heads):
        cols = head_columns(h)
        grad_k = scale * dot(grads_ref[h, B:, :], q_ref[:, cols], ((1,), (0,)))
        grad_v = dot(low_ref[h, B:, :], g_ref[:B, cols], ((1,), (0,)))
        for i, grad in enumerate((grad_k, grad_v)):
            same_ref[i, :, cols] = grad[:pairs]
            other_ref[i, :, cols] = grad[pairs : 2 * pairs].astype(BF16)
    for h in range(heads):
        cols = head_columns(h)
        k = with_summary(k_ref[:, cols], summary_ref, 0, cols, padded)
        gq_ref[:B, cols] = (scale * dot(grads_ref[h], k, ((0,), (0,)))).astype(BF16)


def cross_keys_kernel(heads, q_ref, g_ref, low_ref, grads_ref, gk_ref, gv_ref):
    for h in range(heads):
        cols = head_columns(h)
        gk_ref[:, cols] = E**-0.5 * dot(grads_ref[h, :B, :], q_ref[:, cols], ((1,), (0,)))
        gv_ref[:, cols] = dot(low_ref[h, :B, :], g_ref[:B, cols], ((1,), (0,)))


def final_kernel(
    heads, place_ref, q_ref, g_ref, k_ref, own_ref, weight_ref, gp_ref, top_ref, back_ref,
    gk_ref, gv_ref, gs_ref, out_q_ref, out_k_ref, out_v_ref,
    low, grads, done_q, done_k, done_v, sems
):
    first = place_ref[0] == 0
    scale = E**-0.5
    group = heads // 8 if heads % 8 == 0 else heads
    last_row = lax.broadcasted_iota(jnp.int32, (B, B), 0) == B - 1
    for h in range(heads):
        cols = head_columns(h)
        log_total, inner = stats_of(jnp.where(first, own_ref[:, cols], back_ref[B:, cols]))
        probs = weight_ref[h] * jnp.exp(top_ref[h : h + 1, :] - log_total)
        low[h] = probs.astype(BF16)
        grads[h] = (probs * (gp_ref[h] - inner)).astype(BF16)

    copies = []

    def put(done, out, h):
        if (h + 1) % group == 0:
            part = slice((h + 1 - group) * E, (h + 1) * E)
            sem = sems.at[len(copies)]
            copies.append(pltpu.make_async_copy(done.at[:, part], out.at[:, part], sem))
            copies[-1].start()

    for h in range(heads):
        cols = head_columns(h)
        grad_q = scale * dot(grads[h], k_ref[:, cols], ((0,), (0,)))
        done_q[:, cols] = (grad_q + back_ref[:B, cols].astype(F32)).astype(BF16)
        put(done_q, out_q_ref, h)
    for h in range(heads):
        cols = head_columns(h)
        grad_k = scale * dot(grads[h], q_ref[:, cols], ((1,), (0,)))
        grad_k += gk_ref[:, cols] + jnp.where(last_row, gs_ref[0, :, cols], 0.0)
        done_k[:, cols] = grad_k.astype(BF16)
        put(done_k, out_k_ref, h)
    for h in range(heads):
        cols = head_columns(h)
        grad_v = dot(low[h], g_ref[:, cols], ((1,), (0,)))
        grad_v += gv_ref[:, cols] + jnp.where(last_row, gs_ref[1, :, cols], 0.0)
        done_v[:, cols] = grad_v.astype(BF16)
        put(done_v, out_v_ref, h)
    for copy in copies:
        copy.wait()


def body(queries, key_vectors, value_vectors, grad_out):
    shard_len, features = queries.shape
    count = lax.axis_size("seq")
    assert shard_len == B and count % 2 == 0
    heads = features // E
    place = lax.axis_index("seq").astype(jnp.int32).reshape(1)
    vmem = pl.BlockSpec(memory_space=pltpu.VMEM)
    smem = pl.BlockSpec(memory_space=pltpu.SMEM)
    anywhere = pl.BlockSpec(memory_space=pl.ANY)

    def kernel(
        function,
        name,
        products,
        inputs,
        outputs,
        spec=vmem,
        scratch=(),
        scalar=False,
        source=vmem,
        limit=16 << 20,
    ):
        out_shape = [jax.ShapeDtypeStruct(shape, kind) for shape, kind in outputs]
        moved = sum(x.size * x.dtype.itemsize for x in (*inputs, *out_shape))
        return pl.pallas_call(
            function,
            in_specs=[smem] * scalar + [source] * (len(inputs) - scalar),
            out_specs=[spec] * len(out_shape),
            out_shape=out_shape,
            scratch_shapes=scratch,
            compiler_params=pltpu.CompilerParams(vmem_limit_bytes=limit),
            cost_estimate=pl.CostEstimate(
                flops=products * 2 * heads * B * B * E,
                bytes_accessed=moved,
                transcendentals=heads * B * B,
            ),
            name=name,
        )(*inputs)

    rows = jnp.stack([key_vectors[B - 1 :], value_vectors[B - 1 :]])
    across = [(i, i ^ 1) for i in range(count)]
    swap = lax.ppermute(rows, "seq", across)
    rows, queries = lax.optimization_barrier((rows, queries))
    next_q = passed_round(queries, -1)
    summary = jnp.stack([rows, swap])
    while 2 * summary.shape[2] < count:
        earlier = passed_along(summary, 2 * summary.shape[2])
        summary = jnp.concatenate([summary, earlier], axis=2)
    pairs = summary.shape[2]
    padded = -(-2 * pairs // 16) * 16
    _, grad_out = lax.optimization_barrier((swap, grad_out))
    grad_stats, own_stats = kernel(
        functools.partial(own_kernel, heads),
        "own",
        2,
        (queries, key_vectors, value_vectors, grad_out),
        [
            ((B + STAT_ROWS, features), BF16),
            ((STAT_ROWS, features), BF16),
        ],
        source=anywhere,
        limit=None,
        scratch=[pltpu.VMEM((B, features), BF16)] * 4 + [pltpu.SemaphoreType.DMA((16,))],
    )

    next_g = passed_along(grad_stats, -1)
    grad_out, next_q = lax.optimization_barrier((grad_out, next_q))
    weight, grad_probs, top = kernel(
        functools.partial(own_weights_kernel, heads),
        "own_weights",
        2,
        (queries, key_vectors, value_vectors, grad_out),
        [((heads, B, B), F32)] * 2 + [((heads, B), F32)],
    )

    wide = heads, B + padded, B
    cross_weight, cross_sums = kernel(
        functools.partial(cross_weights_kernel, heads, padded),
        "cross_weights",
        1,
        (place, next_q, key_vectors, summary),
        [(wide, F32), ((2 * heads, B), F32)],
        scalar=True,
    )
    low, grads, same, other, grad_q_next = kernel(
        functools.partial(cross_scores_kernel, heads, padded),
        "cross_scores",
        3,
        (next_q, next_g, key_vectors, value_vectors, summary, cross_weight, cross_sums),
        [(wide, BF16)] * 2
        + [((2, pairs, features), F32), ((2, pairs, features), BF16)]
        + [((B + STAT_ROWS, features), BF16)],
    )
    other = lax.ppermute(other, "seq", across)
    back = passed_along(grad_q_next, 1)
    grad_k, grad_v = kernel(
        functools.partial(cross_keys_kernel, heads),
        "cross_keys",
        2,
        (next_q, next_g, low, grads),
        [((B, features), F32)] * 2,
    )
    grad_summary = same + other.astype(F32)
    while pairs > 1:
        ways = 4 if pairs % 4 == 0 else 2
        pairs //= ways
        parts = [grad_summary[:, i * pairs : (i + 1) * pairs] for i in range(ways)]
        sent = [passed_along(parts[i], -2 * pairs * i) for i in range(1, ways)]
        grad_summary = sum(sent, parts[0])

    return kernel(
        functools.partial(final_kernel, heads),
        "final",
        3,
        (
            place,
            queries,
            grad_out,
            key_vectors,
            own_stats,
            weight,
            grad_probs,
            top,
            back,
            grad_k,
            grad_v,
            grad_summary,
        ),
        [((B, features), BF16)] * 3,
        spec=anywhere,
        scratch=[
            pltpu.VMEM((heads, B, B), BF16),
            pltpu.VMEM((heads, B, B), BF16),
            pltpu.VMEM((B, features), BF16),
            pltpu.VMEM((B, features), BF16),
            pltpu.VMEM((B, features), BF16),
            pltpu.SemaphoreType.DMA((24,)),
        ],
        scalar=True,
    )


def solution(mesh):
    spec = P(("dp", "seq"), "head")
    return jax.shard_map(
        body,
        mesh=mesh,
        in_specs=(spec,) * 4,
        out_specs=(spec,) * 3,
        check_vma=False,
    )
```
